32 devices in a mesh: trow: 4 (over x, core), tcol: 4 (over z), span: 2 (over y).
Axes of the slice: x: 2, y: 2, z: 4, core: 2. Of those that a mesh axis runs over, the one named last changes fastest.
Arguments:
- features: bfloat16 [8, 96, 96, 128], P('span', 'trow', 'tcol'), may hold values from -16 to 16
- norm1_gain: float32 [128], replicated, may hold values from 0.25 to 1.75
- norm1_bias: float32 [128], replicated, may hold values from -3 to 3
- conv1_weight: bfloat16 [3, 3, 3, 128, 128], replicated, may hold values from -0.109375 to 0.109375
- norm2_gain: float32 [128], replicated, may hold values from 0.25 to 1.75
- norm2_bias: float32 [128], replicated, may hold values from -3 to 3
- conv2_weight: bfloat16 [3, 3, 3, 128, 128], replicated, may hold values from -0.109375 to 0.109375
Outputs:
- decoded_video: bfloat16 [8, 96, 96, 128], P('span', 'trow', 'tcol')
The draws below stay inside these ranges and needn't reach their ends.
All inputs are finite; a program needn't handle non-finite values.
Results may differ from the reference program's by a relative error of at most 0.0041.
Values may be sent and summed in bfloat16 or wider, within the bound.
A program may use at most 64 MiB of HBM per device.

```python
import jax
import jax.numpy as jnp
from jax import lax

C = 128
G = 32
S = 24
OV = 8
TILE = 32
FRAMES = 8
HEIGHT = 96
WIDTH = 96
N_TROW = 4
N_TCOL = 4


def draw_features(key, part):
    keys = jax.random.split(key, 3)
    shape = (FRAMES, HEIGHT, WIDTH, C)
    position = jnp.arange(FRAMES, dtype=jnp.float32) / (FRAMES - 1)
    rough = jax.random.uniform(keys[1], (FRAMES, 1, 1, 1), jnp.float32, -0.2, 0.2)
    channel = jnp.exp(jax.random.uniform(keys[2], (1, 1, 1, C), jnp.float32, -0.9, 0.9))
    base = jax.random.normal(keys[0], shape, jnp.float32)
    slope = 0.55
    scale = jnp.exp(slope * position[:, None, None, None] + rough) * channel
    return jnp.clip(base * scale, -16.0, 16.0).astype(jnp.bfloat16)


def noise(own_key, shape, scale, reach, kind=jnp.bfloat16):
    return jnp.clip(scale * jax.random.normal(own_key, shape, jnp.float32), -reach, reach).astype(kind)


def setup_inputs(seed: int = 0) -> dict:
    seeds = jax.random.split(jax.random.key(seed), 8)
    features = draw_features(jax.random.fold_in(seeds[7], 71), 0)
    norm1_gain = jnp.clip(1.0 + 0.15 * jax.random.normal(seeds[1], (C,), jnp.float32), 0.25, 1.75)
    norm1_bias = noise(seeds[2], (C,), 0.5, 3.0, jnp.float32)
    conv1_weight = noise(seeds[3], (3, 3, 3, C, C), (27 * C) ** -0.5, 0.109375)
    norm2_gain = jnp.clip(1.0 + 0.15 * jax.random.normal(seeds[4], (C,), jnp.float32), 0.25, 1.75)
    norm2_bias = noise(seeds[5], (C,), 0.5, 3.0, jnp.float32)
    conv2_weight = noise(seeds[6], (3, 3, 3, C, C), (27 * C) ** -0.5, 0.109375)
    return dict(features=features, norm1_gain=norm1_gain, norm1_bias=norm1_bias, conv1_weight=conv1_weight, norm2_gain=norm2_gain, norm2_bias=norm2_bias, conv2_weight=conv2_weight)


EPSILON = 1e-06

def norm_act(values, gain, bias):
    values = values.astype(jnp.float32)
    group_size = C // G
    grouped = values.reshape(values.shape[:-1] + (G, group_size))
    center = lax.optimization_barrier(jnp.mean(grouped, axis=(0, 1, 2, 4), keepdims=True))
    spread = lax.optimization_barrier(jnp.mean(jnp.square(grouped - center), axis=(0, 1, 2, 4), keepdims=True))
    normed = ((grouped - center) * lax.rsqrt(spread + EPSILON)).reshape(values.shape)
    return jax.nn.silu(normed * gain + bias).astype(jnp.bfloat16)

def causal_conv(acts, weight):
    out_frames = acts.shape[0] - 2
    side_len = acts.shape[1]
    padded = jnp.pad(acts, ((0, 0), (1, 1), (1, 1), (0, 0)), mode='edge')
    totals = jnp.zeros((out_frames * side_len * side_len, weight.shape[4]), jnp.float32)
    for t_off in range(3):
        for r_off in range(3):
            for c_off in range(3):
                window = padded[t_off:t_off + out_frames, r_off:r_off + side_len, c_off:c_off + side_len]
                window = window.reshape(-1, acts.shape[3])
                totals = totals + jnp.dot(window, weight[t_off, r_off, c_off], preferred_element_type=jnp.float32)
    return totals.reshape(out_frames, side_len, side_len, weight.shape[4])

def reference(features, norm1_gain, norm1_bias, conv1_weight, norm2_gain, norm2_bias, conv2_weight):

    def decode_tile(tile_in):
        act_one = norm_act(tile_in, norm1_gain, norm1_bias)
        act_one = jnp.concatenate([act_one[:1], act_one[:1], act_one], axis=0)
        hidden_one = causal_conv(act_one, conv1_weight).astype(jnp.bfloat16)
        act_two = norm_act(hidden_one, norm2_gain, norm2_bias)
        act_two = jnp.concatenate([act_two[:1], act_two[:1], act_two], axis=0)
        hidden_two = causal_conv(act_two, conv2_weight)
        return (tile_in.astype(jnp.float32) + hidden_two).astype(jnp.bfloat16)
    padded = jnp.pad(features, ((0, 0), (0, OV), (0, OV), (0, 0)))
    tiles = jnp.stack([padded[:, row_idx * S:row_idx * S + TILE, col_idx * S:col_idx * S + TILE] for row_idx in range(N_TROW) for col_idx in range(N_TCOL)])
    decoded = lax.map(decode_tile, tiles).reshape(N_TROW, N_TCOL, FRAMES, TILE, TILE, C)
    ramp = jnp.arange(OV, dtype=jnp.float32) / OV
    ramp_rows = ramp[:, None, None]
    top_mix = (decoded[:-1, :, :, S:TILE].astype(jnp.float32) * (1.0 - ramp_rows) + decoded[1:, :, :, :OV].astype(jnp.float32) * ramp_rows).astype(jnp.bfloat16)
    top_rows = jnp.concatenate([decoded[:1, :, :, :OV], top_mix], axis=0)
    vert = jnp.concatenate([top_rows, decoded[:, :, :, OV:S]], axis=3)
    ramp_cols = ramp[:, None]
    side_mix = (vert[:, :-1, :, :, S:TILE].astype(jnp.float32) * (1.0 - ramp_cols) + vert[:, 1:, :, :, :OV].astype(jnp.float32) * ramp_cols).astype(jnp.bfloat16)
    side_cols = jnp.concatenate([vert[:, :1, :, :, :OV], side_mix], axis=1)
    final = jnp.concatenate([side_cols, vert[:, :, :, :, OV:S]], axis=4)
    return final.transpose(2, 0, 3, 1, 4, 5).reshape(FRAMES, N_TROW * S, N_TCOL * S, C)
```

```python
import functools

import jax
import jax.numpy as jnp
from jax import lax
from jax.experimental import pallas as pl
from jax.experimental.pallas import tpu as pltpu
from jax.sharding import PartitionSpec as P

G = 32
OV = 8
EPSILON = 1e-06
F32 = jnp.float32
BF16 = jnp.bfloat16
MESH = pl.DeviceIdType.MESH
ROWS = 8

PREV, R_UP, R_LEFT, R_DIAG, S_UP, S_LEFT, S_DIAG = range(7)
HID = 7
DOWN, RIGHT, CORNER = 16, 18, 20
HALO = 22


def group_sum(x, size):
    lane = lax.broadcasted_iota(jnp.int32, x.shape, 1)
    width = x.shape[1]
    step = 1
    while step < size:
        low = (lane // step) % 2 == 0
        x = x + jnp.where(low, pltpu.roll(x, width - step, 1), pltpu.roll(x, step, 1))
        step *= 2
    return x


def kernel(
    sizes,
    feat,
    gain1_hbm,
    bias1_hbm,
    w1,
    gain2_hbm,
    bias2_hbm,
    w2,
    out,
    own,
    halo_b,
    halo_r,
    halo_c,
    tile,
    acts,
    hid,
    wp1,
    wp2,
    send_d,
    send_r,
    send_c,
    recv_d,
    recv_r,
    recv_c,
    stat_tx,
    stat_rx,
    send_sem,
    recv_sem,
    st_send,
    st_recv,
    w_sem,
    own_sem,
    gain1,
    bias1,
    gain2,
    bias2,
    param_sem,
    piece_tx,
    piece_rx,
):
    n_row, n_col, n_span = sizes
    frames, stride, _, chan = feat.shape
    side = stride + OV
    steps = side // ROWS
    group = chan // G
    row, col, span = (lax.axis_index(a) for a in ("trow", "tcol", "span"))
    has_up, has_down = row > 0, row < n_row - 1
    has_left, has_right = col > 0, col < n_col - 1
    is_first, has_next = span == 0, span < n_span - 1

    def dev(dr, dc, ds):
        return {
            "trow": lax.rem(row + dr + n_row, n_row),
            "tcol": lax.rem(col + dc + n_col, n_col),
            "span": lax.rem(span + ds + n_span, n_span),
        }

    def remote(src, dst, k, dr, dc, ds):
        return pltpu.make_async_remote_copy(
            src_ref=src,
            dst_ref=dst,
            send_sem=send_sem.at[k],
            recv_sem=recv_sem.at[k],
            device_id=dev(dr, dc, ds),
            device_id_type=MESH,
        )

    barrier = pltpu.get_barrier_semaphore()
    i32 = jnp.int32
    near = [
        (has_up, -1, 0),
        (has_down, 1, 0),
        (has_left, 0, -1),
        (has_right, 0, 1),
        (jnp.logical_and(has_up, has_left), -1, -1),
        (jnp.logical_and(has_down, has_right), 1, 1),
    ]
    count = jnp.asarray(n_span - 1, i32)
    for cond, dr, dc in near:

        @pl.when(cond)
        def _():
            pl.semaphore_signal(barrier, inc=1, device_id=dev(dr, dc, 0), device_id_type=MESH)

        count = count + cond.astype(i32)
    for j in range(1, n_span):
        pl.semaphore_signal(barrier, inc=1, device_id=dev(0, 0, j), device_id_type=MESH)

    own_copy = pltpu.make_async_copy(feat, own.at[2 : 2 + frames], own_sem)
    own_copy.start()
    p_copies = [
        pltpu.make_async_copy(src, dst, param_sem.at[k])
        for k, (src, dst) in enumerate(
            ((gain1_hbm, gain1), (bias1_hbm, bias1), (gain2_hbm, gain2), (bias2_hbm, bias2))
        )
    ]
    for c in p_copies:
        c.start()
    w_copies = []
    for n, (w, wp) in enumerate(((w1, wp1), (w2, wp2))):
        for kt in range(3):
            for o in range(2):
                k = (kt + o) * 3 * chan
                w_copies.append(
                    pltpu.make_async_copy(
                        w.at[kt],
                        wp.at[:, k : k + 3 * chan, o * chan : (o + 1) * chan],
                        w_sem.at[n * 6 + kt * 2 + o],
                    )
                )
    for c in w_copies:
        c.start()
    pl.semaphore_wait(barrier, count)

    def when(cond, fn):
        @pl.when(cond)
        def _():
            fn()

    both_ul = jnp.logical_and(has_up, has_left)
    both_dr = jnp.logical_and(has_down, has_right)
    c_up, c_left, c_diag = [], [], []
    for f in range(frames):
        k = HALO + 3 * f
        c_left.append(remote(feat.at[f, :, 0:OV], halo_r.at[2 + f], k, 0, -1, 0))
        c_up.append(remote(feat.at[f, 0:OV], halo_b.at[2 + f], k + 1, -1, 0, 0))
        c_diag.append(remote(feat.at[f, 0:OV, 0:OV], halo_c.at[2 + f], k + 2, -1, -1, 0))
    p_top = remote(piece_tx.at[0], piece_rx.at[0], S_UP, -1, 0, 0)
    p_left = remote(piece_tx.at[1], piece_rx.at[1], S_LEFT, 0, -1, 0)
    p_diag = remote(piece_tx.at[2], piece_rx.at[2], S_DIAG, -1, -1, 0)
    c_prev = remote(feat.at[frames - 2 : frames], own.at[0:2], PREV, 0, 0, 1)
    r_up = remote(own.at[0:2, 0:OV], halo_b.at[0:2], R_UP, -1, 0, 0)
    r_left = remote(own.at[0:2, :, 0:OV], halo_r.at[0:2], R_LEFT, 0, -1, 0)
    r_diag = remote(own.at[0:2, 0:OV, 0:OV], halo_c.at[0:2], R_DIAG, -1, -1, 0)

    def start_halos(chosen):
        for f in chosen:
            when(has_left, c_left[f].start)
            when(both_ul, c_diag[f].start)
            when(has_up, c_up[f].start)


    def zero(ref):
        ref[...] = jnp.zeros(ref.shape, ref.dtype)

    when(jnp.logical_not(has_down), lambda: zero(halo_b))
    when(jnp.logical_not(has_right), lambda: zero(halo_r))
    when(jnp.logical_not(both_dr), lambda: zero(halo_c))
    when(jnp.logical_not(has_down), lambda: zero(piece_rx.at[0]))
    when(jnp.logical_not(has_right), lambda: zero(piece_rx.at[1]))
    when(jnp.logical_not(both_dr), lambda: zero(piece_rx.at[2]))
    for wp in (wp1, wp2):
        wp[:, 0 : 3 * chan, chan:] = jnp.zeros((3, 3 * chan, chan), BF16)
        wp[:, 9 * chan : 12 * chan, 0:chan] = jnp.zeros((3, 3 * chan, chan), BF16)

    def assemble(f):
        for r in range(0, stride, 8):
            part = jnp.concatenate(
                [own[f, r : r + 8].astype(F32), halo_r[f, r : r + 8].astype(F32)], axis=1
            )
            tile[f, r : r + 8] = part.astype(BF16)
        part = jnp.concatenate([halo_b[f].astype(F32), halo_c[f].astype(F32)], axis=1)
        tile[f, stride:side] = part.astype(BF16)

    members = frames * side * side * group

    def rows8(parts):
        parts = list(parts)
        pad = jnp.zeros((8 - len(parts), chan), F32)
        return jnp.concatenate(parts + [pad], axis=0)

    def merge(pieces):
        n = sum(p[0] for p in pieces)
        mean = sum(p[1] * (p[0] / n) for p in pieces)
        dev = sum(p[2] + p[0] * (p[1] - mean) * (p[1] - mean) for p in pieces)
        return n, mean, dev

    def quarters(f):
        x = own[f].astype(F32)
        return (
            x[0:OV, 0:OV],
            x[0:OV, OV:stride],
            x[OV:stride, 0:OV],
            x[OV:stride, OV:stride],
        )

    def fold8(x):
        return jnp.sum(x.reshape(-1, 8, chan), axis=0)

    inner = stride - OV
    counts = [frames * group * a for a in (OV * OV, OV * inner, inner * OV, inner * inner)]
    none = tuple(jnp.zeros((8, chan), F32) for _ in range(4))
    own_copy.wait()
    for c in p_copies:
        c.wait()
    sums = lax.fori_loop(
        2, 2 + frames, lambda f, t: tuple(a + fold8(q) for a, q in zip(t, quarters(f))), none
    )
    means = group_sum(
        rows8(jnp.sum(t, axis=0, keepdims=True) * (1.0 / n) for t, n in zip(sums, counts)), group
    )

    def deviations(f, t):
        result = []
        for i, q in enumerate(quarters(f)):
            off = q - means[i : i + 1][None]
            result.append(t[i] + fold8(off * off))
        return tuple(result)

    devs = lax.fori_loop(2, 2 + frames, deviations, none)
    devs = group_sum(rows8(jnp.sum(t, axis=0, keepdims=True) for t in devs), group)
    quads = [(n, means[i : i + 1], devs[i : i + 1]) for i, n in enumerate(counts)]
    for k, piece in enumerate((merge(quads[0:2]), merge([quads[0], quads[2]]), quads[0])):
        piece_tx[k] = rows8(piece[1:])
    when(has_up, p_top.start)
    when(has_left, p_left.start)
    when(both_ul, p_diag.start)
    start_halos(range(frames))
    when(has_next, c_prev.start)
    when(has_down, p_top.wait_recv)
    when(has_right, p_left.wait_recv)
    when(both_dr, p_diag.wait_recv)
    got = [
        (n, piece_rx[k, 0:1], piece_rx[k, 1:2])
        for k, n in enumerate((counts[0] + counts[1], counts[0] + counts[2], counts[0]))
    ]
    _, tile_mean, tile_dev = merge([merge(quads)] + got)

    def mean_of(t):
        s = jnp.sum(t, axis=0, keepdims=True)
        return group_sum(jnp.broadcast_to(s, (8, chan)), group) * (1.0 / members)

    def spread_of(ref, center):
        def step(i, t):
            f = 2 + i // steps
            r = (i % steps) * ROWS
            off = ref[f, pl.ds(r, ROWS)].astype(F32) - center[0:1][None]
            off = off * off
            return t + jnp.sum(off.reshape(-1, 8, chan), axis=0)

        t = lax.fori_loop(0, frames * steps, step, jnp.zeros((8, chan), F32))
        s = jnp.sum(t, axis=0, keepdims=True)
        return group_sum(jnp.broadcast_to(s, (8, chan)), group)

    def exchange(n, center, spread):
        stat_tx[n, 0] = center
        stat_tx[n, 1] = spread
        copies = []
        for j in range(1, n_span):
            c = pltpu.make_async_remote_copy(
                src_ref=stat_tx.at[n],
                dst_ref=stat_rx.at[n, j - 1],
                send_sem=st_send.at[n, j - 1],
                recv_sem=st_recv.at[n, j - 1],
                device_id=dev(0, 0, j),
                device_id_type=MESH,
            )
            c.start()
            copies.append(c)
        for c in copies:
            c.wait()
        total = center
        for j in range(n_span - 1):
            total = total + stat_rx[n, j, 0]
        mean = total * (1.0 / n_span)
        dev2 = spread + members * (center - mean) * (center - mean)
        for j in range(n_span - 1):
            d = stat_rx[n, j, 0] - mean
            dev2 = dev2 + stat_rx[n, j, 1] + members * d * d
        return mean, lax.rsqrt(dev2 * (1.0 / (members * n_span)) + EPSILON)

    def activate(ref, f, mean, scale, bias):
        base = f * 3 * chan

        def step(i, carry):
            r = i * ROWS
            x = ref[f, pl.ds(r, ROWS)].astype(F32)
            u = (x - mean[0:1][None]) * scale[0:1][None] + bias[None]
            y = u * jnp.tanh(u) + u
            left = jnp.concatenate([y[:, 0:1], y[:, 0 : side - 1]], axis=1)
            right = jnp.concatenate([y[:, 1:side], y[:, side - 1 : side]], axis=1)
            rows = pl.ds(r + 1, ROWS)
            acts[rows, :, base : base + chan] = left.astype(BF16)
            acts[rows, :, base + chan : base + 2 * chan] = y.astype(BF16)
            acts[rows, :, base + 2 * chan : base + 3 * chan] = right.astype(BF16)
            return carry

        lax.fori_loop(0, steps, step, 0)
        lanes = slice(base, base + 3 * chan)
        acts[0, :, lanes] = acts[1, :, lanes]
        acts[side + 1, :, lanes] = acts[side, :, lanes]

    def conv_rows(wp, first, r):
        base = first * 3 * chan
        acc = None
        for kh in range(3):
            lhs = acts[pl.ds(r + kh, ROWS), :, base : base + 12 * chan]
            part = jnp.dot(
                lhs.reshape(ROWS * side, 12 * chan), wp[kh], preferred_element_type=F32
            )
            acc = part if acc is None else acc + part
        return acc

    def hid_copy(r):
        k = HID + r // ROWS
        rows = pl.ds(r, ROWS)
        return remote(hid.at[frames : frames + 2, rows], hid.at[0:2, rows], k, 0, 0, 1)

    def conv1(first, lo, hi, send, total):
        def step(i, carry):
            r = i * ROWS
            acc = conv_rows(wp1, first, r)
            for o in range(2):
                part = acc[:, o * chan : (o + 1) * chan].reshape(ROWS, side, chan).astype(BF16)
                hid[first + 2 + o, pl.ds(r, ROWS)] = part
                carry = carry + fold8(part.astype(F32))
            if send:
                when(has_next, lambda: hid_copy(r).start())
            return carry

        return lax.fori_loop(lo, hi, step, total)

    mean, inv = exchange(
        0, jnp.broadcast_to(tile_mean, (8, chan)), jnp.broadcast_to(tile_dev, (8, chan))
    )
    scale = inv * (0.5 * gain1[...])
    half_bias = 0.5 * bias1[...]
    for f in range(frames):
        when(has_right, c_left[f].wait_recv)
        when(both_dr, c_diag[f].wait_recv)
        when(has_down, c_up[f].wait_recv)
        assemble(2 + f)
        activate(tile, 2 + f, mean, scale, half_bias)
    for c in w_copies[:6]:
        c.wait()
    totals = conv1(frames - 2, 0, steps // 2, True, jnp.zeros((8, chan), F32))

    later = jnp.logical_not(is_first)

    @pl.when(later)
    def _():
        c_prev.wait_recv()
        when(has_up, r_up.start)
        when(has_left, r_left.start)
        when(both_ul, r_diag.start)

    totals = conv1(frames - 2, steps // 2, steps, True, totals)

    @pl.when(later)
    def _():
        when(has_down, r_up.wait_recv)
        when(has_right, r_left.wait_recv)
        when(both_dr, r_diag.wait_recv)
        for f in range(2):
            assemble(f)

    @pl.when(is_first)
    def _():
        for f in range(2):
            tile[f] = tile[2]

    for f in range(2):
        activate(tile, f, mean, scale, half_bias)
    totals = conv1(0, 0, steps, False, totals)

    center = mean_of(totals)
    mean, inv = exchange(1, center, spread_of(hid, center))
    scale = inv * (0.5 * gain2[...])
    half_bias = 0.5 * bias2[...]
    for f in range(2, 2 + frames):
        activate(hid, f, mean, scale, half_bias)
    for c in w_copies[6:]:
        c.wait()

    def edge_copies(first):
        p = first // 2
        two = pl.ds(first, 2)
        return (
            remote(send_d.at[two], recv_d.at[two], DOWN + p, 1, 0, 0),
            remote(send_r.at[two], recv_r.at[two], RIGHT + p, 0, 1, 0),
            remote(send_c.at[two], recv_c.at[two], CORNER + p, 1, 1, 0),
        )

    def conv2(first):
        d_copy, r_copy, c_copy = edge_copies(first)

        def decoded(r):
            acc = conv_rows(wp2, first, r)
            parts = []
            for o in range(2):
                f = first + o
                part = acc[:, o * chan : (o + 1) * chan].reshape(ROWS, side, chan)
                parts.append(part + tile[f + 2, pl.ds(r, ROWS)].astype(F32))
            return parts

        def step(i, carry):
            r = side - ROWS - i * ROWS
            for o, part in enumerate(decoded(r)):
                f = first + o

                @pl.when(i == 0)
                def _():
                    send_d[f] = part[:, 0:stride].astype(BF16)
                    send_c[f] = part[:, stride:side].astype(BF16)

                @pl.when(i > 0)
                def _():
                    rows = pl.ds(jnp.minimum(r, stride - ROWS), ROWS)
                    out[f, rows] = part[:, 0:stride].astype(BF16)
                    send_r[f, rows] = part[:, stride:side].astype(BF16)

            @pl.when(i == 0)
            def _():
                when(has_down, d_copy.start)
                when(both_dr, c_copy.start)

            return carry

        lax.fori_loop(0, steps, step, 0)
        when(has_right, r_copy.start)

    ramp = lax.broadcasted_iota(jnp.int32, (1, OV, 1), 1).astype(F32) * (1.0 / OV)

    def blend(first):
        d_copy, r_copy, c_copy = edge_copies(first)
        when(has_up, d_copy.wait_recv)
        when(has_left, r_copy.wait_recv)
        when(both_ul, c_copy.wait_recv)

        @pl.when(has_up)
        def _():
            for f in (first, first + 1):
                for i in range(OV):
                    t = i / OV
                    mix = recv_d[f, i].astype(F32) * (1.0 - t) + out[f, i].astype(F32) * t
                    out[f, i] = mix.astype(BF16)

        @pl.when(both_ul)
        def _():
            for f in (first, first + 1):
                for i in range(OV):
                    t = i / OV
                    mix = recv_c[f, i].astype(F32) * (1.0 - t) + recv_r[f, i].astype(F32) * t
                    recv_r[f, i] = mix.astype(BF16)

        @pl.when(has_left)
        def _():
            for f in (first, first + 1):
                for r in range(0, stride, 8):
                    rows = slice(r, r + 8)
                    mine = out[f, rows].astype(F32)
                    mix = recv_r[f, rows].astype(F32) * (1.0 - ramp) + mine[:, 0:OV] * ramp
                    out[f, rows] = jnp.concatenate([mix, mine[:, OV:]], axis=1).astype(BF16)

    conv2(frames - 2)

    @pl.when(later)
    def _():
        for i in range(steps):
            hid_copy(i * ROWS).wait_recv()

    @pl.when(is_first)
    def _():
        for f in range(2):
            hid[f] = hid[2]

    for f in range(2):
        activate(hid, f, mean, scale, half_bias)
    conv2(0)
    blend(frames - 2)
    blend(0)

    for f in range(frames):
        when(has_left, c_left[f].wait_send)
        when(both_ul, c_diag[f].wait_send)
        when(has_up, c_up[f].wait_send)
    when(has_up, p_top.wait_send)
    when(has_left, p_left.wait_send)
    when(both_ul, p_diag.wait_send)

    @pl.when(has_next)
    def _():
        c_prev.wait_send()
        for i in range(steps):
            hid_copy(i * ROWS).wait_send()

    @pl.when(later)
    def _():
        when(has_up, r_up.wait_send)
        when(has_left, r_left.wait_send)
        when(both_ul, r_diag.wait_send)

    for first in (0, frames - 2):
        d_copy, r_copy, c_copy = edge_copies(first)
        when(has_down, d_copy.wait_send)
        when(has_right, r_copy.wait_send)
        when(both_dr, c_copy.wait_send)


def store(src, dst, sem):
    copy = pltpu.make_async_copy(src, dst, sem)
    copy.start()
    copy.wait()


def body(sizes, features, norm1_gain, norm1_bias, conv1_weight, norm2_gain, norm2_bias, conv2_weight):
    frames, stride, _, chan = features.shape
    side = stride + OV
    n_other = max(sizes[2] - 1, 1)
    vmem = pl.BlockSpec(memory_space=pltpu.VMEM)
    hbm = pl.BlockSpec(memory_space=pltpu.HBM)
    flat = lambda v: v.reshape(1, chan)
    taps = lambda w: w.reshape(3, 3, 3 * chan, chan)
    flops = 2 * 2 * frames * side * side * 27 * chan * chan
    result = pl.pallas_call(
        functools.partial(kernel, sizes),
        out_shape=pltpu.VMEM(features.shape, BF16),
        in_specs=[hbm] * 7,
        out_specs=vmem,
        scratch_shapes=[
            pltpu.VMEM((frames + 2, stride, stride, chan), BF16),
            pltpu.VMEM((frames + 2, OV, stride, chan), BF16),
            pltpu.VMEM((frames + 2, stride, OV, chan), BF16),
            pltpu.VMEM((frames + 2, OV, OV, chan), BF16),
            pltpu.VMEM((frames + 2, side, side, chan), BF16),
            pltpu.VMEM((side + 2, side, (frames + 2) * 3 * chan), BF16),
            pltpu.VMEM((frames + 2, side, side, chan), BF16),
            pltpu.VMEM((3, 12 * chan, 2 * chan), BF16),
            pltpu.VMEM((3, 12 * chan, 2 * chan), BF16),
            pltpu.VMEM((frames, OV, stride, chan), BF16),
            pltpu.VMEM((frames, stride, OV, chan), BF16),
            pltpu.VMEM((frames, OV, OV, chan), BF16),
            pltpu.VMEM((frames, OV, stride, chan), BF16),
            pltpu.VMEM((frames, stride, OV, chan), BF16),
            pltpu.VMEM((frames, OV, OV, chan), BF16),
            pltpu.VMEM((2, 2, 8, chan), F32),
            pltpu.VMEM((2, n_other, 2, 8, chan), F32),
            pltpu.SemaphoreType.DMA((HALO + 3 * frames,)),
            pltpu.SemaphoreType.DMA((HALO + 3 * frames,)),
            pltpu.SemaphoreType.DMA((2, n_other)),
            pltpu.SemaphoreType.DMA((2, n_other)),
            pltpu.SemaphoreType.DMA((12,)),
            pltpu.SemaphoreType.DMA,
            *[pltpu.VMEM((1, chan), F32) for _ in range(4)],
            pltpu.SemaphoreType.DMA((4,)),
            pltpu.VMEM((3, 8, chan), F32),
            pltpu.VMEM((3, 8, chan), F32),
        ],
        compiler_params=pltpu.CompilerParams(
            collective_id=0, has_side_effects=True, vmem_limit_bytes=40_000_000
        ),
        cost_estimate=pl.CostEstimate(
            flops=flops, bytes_accessed=4 << 20, transcendentals=12 * side * side * chan
        ),
    )(
        *[
            pltpu.with_memory_space_constraint(v, pltpu.HBM)
            for v in (
                features,
                flat(norm1_gain),
                flat(norm1_bias),
                taps(conv1_weight),
                flat(norm2_gain),
                flat(norm2_bias),
                taps(conv2_weight),
            )
        ]
    )
    return result


def solution(mesh):
    sizes = tuple(mesh.shape[a] for a in ("trow", "tcol", "span"))
    placed = (P("span", "trow", "tcol", None), P(), P(), P(), P(), P(), P())
    return jax.shard_map(
        functools.partial(body, sizes),
        mesh=mesh,
        in_specs=placed,
        out_specs=P("span", "trow", "tcol", None),
        check_vma=False,
    )
```

```python
import functools

import jax
import jax.numpy as jnp
from jax import lax
from jax.experimental import pallas as pl
from jax.experimental.pallas import tpu as pltpu
from jax.sharding import PartitionSpec as P

G = 32
OV = 8
EPSILON = 1e-06
F32 = jnp.float32
BF16 = jnp.bfloat16
MESH = pl.DeviceIdType.MESH
ROWS = 8

UP, LIFT, LEFT = 0, 1, 2
PREV, R_UP, R_DIAG, R_LEFT = 5, 8, 9, 10
HID = 11
DOWN, CORNER, RIGHT = 15, 17, 19
N_SEM = 21
FULL, TOP, SIDE, BOTH = range(4)


def group_sum(x, size):
    lane = lax.broadcasted_iota(jnp.int32, x.shape, 1)
    width = x.shape[1]
    step = 1
    while step < size:
        low = (lane // step) % 2 == 0
        x = x + jnp.where(low, pltpu.roll(x, width - step, 1), pltpu.roll(x, step, 1))
        step *= 2
    return x


def kernel(
    sizes,
    feat,
    gain1_hbm,
    bias1_hbm,
    w1,
    gain2_hbm,
    bias2_hbm,
    w2,
    out,
    own,
    halo_b,
    halo_r,
    halo_c,
    tile,
    acts,
    hid,
    wp1,
    wp2,
    send_d,
    send_r,
    send_c,
    recv_d,
    recv_r,
    recv_c,
    hid_mean,
    hid_dev,
    piece_tx,
    piece_rx,
    stat_tx,
    stat_rx,
    send_sem,
    recv_sem,
    piece_send,
    piece_recv,
    stat_send,
    stat_recv,
    w_sem,
    own_sem,
    gain1,
    bias1,
    gain2,
    bias2,
    param_sem,
):
    n_row, n_col, n_span = sizes
    frames, stride, _, chan = feat.shape
    side = stride + OV
    steps = side // ROWS
    group = chan // G
    row, col, span = (lax.axis_index(a) for a in ("trow", "tcol", "span"))
    has_up, has_down = row > 0, row < n_row - 1
    has_left, has_right = col > 0, col < n_col - 1
    both_ul = jnp.logical_and(has_up, has_left)
    both_dr = jnp.logical_and(has_down, has_right)
    is_first, later, has_next = span == 0, span > 0, span < n_span - 1

    def dev(dr, dc, ds):
        return {
            "trow": lax.rem(row + dr + n_row, n_row),
            "tcol": lax.rem(col + dc + n_col, n_col),
            "span": lax.rem(span + ds + n_span, n_span),
        }

    def remote(src, dst, k, dr, dc, ds):
        return pltpu.make_async_remote_copy(
            src_ref=src,
            dst_ref=dst,
            send_sem=send_sem.at[k],
            recv_sem=recv_sem.at[k],
            device_id=dev(dr, dc, ds),
            device_id_type=MESH,
        )

    def when(cond, fn):
        @pl.when(cond)
        def _():
            fn()

    own_copy = pltpu.make_async_copy(feat, own.at[2 : 2 + frames], own_sem)
    own_copy.start()
    barrier = pltpu.get_barrier_semaphore()
    near = [
        (has_up, -1, 0),
        (has_down, 1, 0),
        (has_left, 0, -1),
        (has_right, 0, 1),
        (both_ul, -1, -1),
        (both_dr, 1, 1),
    ]

    def greet(dr, dc, ds):
        pl.semaphore_signal(barrier, inc=1, device_id=dev(dr, dc, ds), device_id_type=MESH)

    count = jnp.asarray(n_span - 1, jnp.int32)
    for cond, dr, dc in near:

        @pl.when(cond)
        def _():
            for j in range(n_span):
                greet(dr, dc, j)

        count = count + cond.astype(jnp.int32) * n_span
    for j in range(1, n_span):
        greet(0, 0, j)

    members = frames * side * side

    def rows8(parts):
        parts = list(parts)
        pad = jnp.zeros((8 - len(parts), chan), F32)
        return jnp.concatenate(parts + [pad], axis=0)

    def merge(pieces):
        n = sum(p[0] for p in pieces)
        mean = sum(p[1] * (p[0] / n) for p in pieces)
        dev = sum(p[2] + p[0] * (p[1] - mean) * (p[1] - mean) for p in pieces)
        return n, mean, dev

    def quarters(f):
        x = own[f].astype(F32)
        return (
            x[0:OV, 0:OV],
            x[0:OV, OV:stride],
            x[OV:stride, 0:OV],
            x[OV:stride, OV:stride],
        )

    def fold8(x):
        return jnp.sum(x.reshape(-1, 8, chan), axis=0)

    inner = stride - OV
    counts = [frames * a for a in (OV * OV, OV * inner, inner * OV, inner * inner)]
    none = tuple(jnp.zeros((8, chan), F32) for _ in range(4))
    own_copy.wait()
    sums = lax.fori_loop(
        2, 2 + frames, lambda f, t: tuple(a + fold8(q) for a, q in zip(t, quarters(f))), none
    )
    means = [jnp.sum(t, axis=0, keepdims=True) * (1.0 / n) for t, n in zip(sums, counts)]

    def deviations(f, t):
        result = []
        for i, q in enumerate(quarters(f)):
            off = q - means[i][None]
            result.append(t[i] + fold8(off * off))
        return tuple(result)

    devs = lax.fori_loop(2, 2 + frames, deviations, none)
    devs = [jnp.sum(t, axis=0, keepdims=True) for t in devs]
    quads = list(zip(counts, means, devs))
    mine = [merge(quads), merge(quads[0:2]), merge([quads[0], quads[2]]), quads[0]]
    for k, piece in enumerate(mine):
        piece_tx[k] = rows8(piece[1:])

    sent, arrives = [], []
    for j in range(n_span):
        for k, goes, comes, dr, dc in (
            (FULL, None, None, 0, 0),
            (TOP, has_up, has_down, -1, 0),
            (SIDE, has_left, has_right, 0, -1),
            (BOTH, both_ul, both_dr, -1, -1),
        ):
            if j == 0 and k == FULL:
                continue
            c = pltpu.make_async_remote_copy(
                src_ref=piece_tx.at[k],
                dst_ref=piece_rx.at[j, k],
                send_sem=piece_send.at[j, k],
                recv_sem=piece_recv.at[j, k],
                device_id=dev(dr, dc, j),
                device_id_type=MESH,
            )
            sent.append((goes, c))
            arrives.append((comes, c))

    def maybe(cond, fn):
        if cond is None:
            fn()
        else:
            when(cond, fn)

    pl.semaphore_wait(barrier, count)
    for cond, c in sent:
        maybe(cond, c.start)

    mid = slice(2, 2 + frames)
    c_up = remote(feat.at[:, 0:OV], halo_b.at[mid], UP, -1, 0, 0)
    c_lift = remote(halo_r.at[mid, 0:OV], halo_c.at[mid], LIFT, -1, 0, 0)

    def c_left(i):
        rows = pl.ds(i * ROWS, ROWS)
        return remote(feat.at[:, rows, 0:OV], halo_r.at[mid, rows], LEFT + i, 0, -1, 0)

    n_left = stride // ROWS

    def c_prev(i):
        rows, cols = (
            (slice(0, stride), slice(0, OV)),
            (slice(0, OV), slice(OV, stride)),
            (slice(OV, stride), slice(OV, stride)),
        )[i]
        src = feat.at[frames - 2 : frames, rows, cols]
        return remote(src, own.at[0:2, rows, cols], PREV + i, 0, 0, 1)

    r_up = remote(own.at[0:2, 0:OV], halo_b.at[0:2], R_UP, -1, 0, 0)
    r_diag = remote(own.at[0:2, 0:OV, 0:OV], halo_c.at[0:2], R_DIAG, -1, -1, 0)
    r_left = remote(own.at[0:2, :, 0:OV], halo_r.at[0:2], R_LEFT, 0, -1, 0)

    @pl.when(has_next)
    def _():
        for i in range(3):
            c_prev(i).start()

    @pl.when(has_left)
    def _():
        for i in range(n_left):
            c_left(i).start()

    when(has_up, c_up.start)
    p_copies = [
        pltpu.make_async_copy(src, dst, param_sem.at[k])
        for k, (src, dst) in enumerate(
            ((gain1_hbm, gain1), (bias1_hbm, bias1), (gain2_hbm, gain2), (bias2_hbm, bias2))
        )
    ]
    for c in p_copies:
        c.start()
    w_copies = []
    for n, (w, wp) in enumerate(((w1, wp1), (w2, wp2))):
        for kt in range(3):
            for o in range(2):
                k = (kt + o) * 3 * chan
                w_copies.append(
                    pltpu.make_async_copy(
                        w.at[kt],
                        wp.at[:, k : k + 3 * chan, o * chan : (o + 1) * chan],
                        w_sem.at[n * 6 + kt * 2 + o],
                    )
                )
    for c in w_copies:
        c.start()

    def zero(ref):
        ref[...] = jnp.zeros(ref.shape, ref.dtype)

    when(jnp.logical_not(has_down), lambda: zero(halo_b))
    when(jnp.logical_not(has_right), lambda: zero(halo_r))
    when(jnp.logical_not(both_dr), lambda: zero(halo_c))
    for j in range(n_span):
        when(jnp.logical_not(has_down), lambda: zero(piece_rx.at[j, TOP]))
        when(jnp.logical_not(has_right), lambda: zero(piece_rx.at[j, SIDE]))
        when(jnp.logical_not(both_dr), lambda: zero(piece_rx.at[j, BOTH]))
    for wp in (wp1, wp2):
        wp[:, 0 : 3 * chan, chan:] = jnp.zeros((3, 3 * chan, chan), BF16)
        wp[:, 9 * chan : 12 * chan, 0:chan] = jnp.zeros((3, 3 * chan, chan), BF16)

    def assemble(f, r):
        rows = pl.ds(r, ROWS)
        part = jnp.concatenate([own[f, rows].astype(F32), halo_r[f, rows].astype(F32)], axis=1)
        tile[f, rows] = part.astype(BF16)

    def assemble_low(f):
        part = jnp.concatenate([halo_b[f].astype(F32), halo_c[f].astype(F32)], axis=1)
        tile[f, stride:side] = part.astype(BF16)

    def coefficients(mean, dev2, gain, bias):
        wide = lambda v: jnp.broadcast_to(v, (8, chan))
        center = group_sum(wide(mean), group) * (1.0 / group)
        off = mean - center
        spread = group_sum(wide(dev2) + (members * n_span) * off * off, group)
        inv = lax.rsqrt(spread * (1.0 / (members * group * n_span)) + EPSILON)
        scale = inv[0:1] * (0.5 * gain[...])
        return scale, 0.5 * bias[...] - center[0:1] * scale

    def activate(ref, src, f, r, norm):
        scale, shift = norm
        base = f * 3 * chan
        x = ref[src, pl.ds(r, ROWS)].astype(F32)
        u = x * scale[None] + shift[None]
        y = u * jnp.tanh(u) + u
        left = jnp.concatenate([y[:, 0:1], y[:, 0 : side - 1]], axis=1)
        right = jnp.concatenate([y[:, 1:side], y[:, side - 1 : side]], axis=1)
        rows = pl.ds(r + 1, ROWS)
        acts[rows, :, base : base + chan] = left.astype(BF16)
        acts[rows, :, base + chan : base + 2 * chan] = y.astype(BF16)
        acts[rows, :, base + 2 * chan : base + 3 * chan] = right.astype(BF16)

    def close_top(lo, hi):
        lanes = slice(lo * 3 * chan, hi * 3 * chan)
        acts[0, :, lanes] = acts[1, :, lanes]

    def close_bottom(lo, hi):
        lanes = slice(lo * 3 * chan, hi * 3 * chan)
        acts[side + 1, :, lanes] = acts[side, :, lanes]

    def conv_block(wp, first, r, rows, c, cols):
        base = first * 3 * chan
        acc = None
        for kh in range(3):
            lhs = acts[pl.ds(r + kh, rows), c : c + cols, base : base + 12 * chan]
            part = jnp.dot(
                lhs.reshape(rows * cols, 12 * chan), wp[kh], preferred_element_type=F32
            )
            acc = part if acc is None else acc + part
        return [acc[:, o * chan : (o + 1) * chan].reshape(rows, cols, chan) for o in range(2)]

    def hid_copy(i):
        rows = pl.ds(i * ROWS, ROWS)
        return remote(hid.at[frames : frames + 2, rows], hid.at[0:2, rows], HID + i, 0, 0, 1)

    def keep_hidden(first, r, rows, slot):
        parts = [p.astype(BF16) for p in conv_block(wp1, first, r, rows, 0, side)]
        wide = []
        for o, part in enumerate(parts):
            hid[first + 2 + o, pl.ds(r, rows)] = part
            wide.append(part.astype(F32))
        center = (fold8(wide[0]) + fold8(wide[1])) * (8.0 / (2 * rows * side))
        off = [(w.reshape(-1, 8, chan) - center[None]) for w in wide]
        hid_mean[slot] = center
        hid_dev[slot] = fold8(off[0] * off[0]) + fold8(off[1] * off[1])

    for c in p_copies:
        c.wait()
    for cond, c in arrives:
        maybe(cond, c.wait_recv)
    area = [frames * a for a in (stride * stride, OV * stride, stride * OV, OV * OV)]
    pieces = [mine[FULL]]
    for j in range(n_span):
        for k in range(4):
            if j or k:
                pieces.append((area[k], piece_rx[j, k, 0:1], piece_rx[j, k, 1:2]))
    _, mean, dev2 = merge(pieces)
    norm = coefficients(mean, dev2, gain1, bias1)

    middle = range(2, 2 + frames)
    can_lift = jnp.logical_and(has_up, has_right)
    when(has_right, c_left(0).wait_recv)
    when(can_lift, c_lift.start)
    for f in middle:
        assemble(f, 0)
        activate(tile, f, f, 0, norm)
    close_top(2, 2 + frames)
    for c in w_copies[:6]:
        c.wait()

    last = frames - 2

    def first_pair(k, carry):
        n = k + 1

        @pl.when(n < n_left)
        def _():
            when(has_right, c_left(n).wait_recv)
            for f in middle:
                assemble(f, n * ROWS)

        @pl.when(n == n_left)
        def _():
            when(has_down, c_up.wait_recv)
            when(both_dr, c_lift.wait_recv)
            for f in middle:
                assemble_low(f)

        @pl.when(n < steps)
        def _():
            for f in middle:
                activate(tile, f, f, n * ROWS, norm)

        when(n == n_left, lambda: close_bottom(2, 2 + frames))
        keep_hidden(last, k * ROWS, ROWS, k)
        when(jnp.logical_and(has_next, k < steps // 2), hid_copy(k).start)

        @pl.when(jnp.logical_and(later, k == 0))
        def _():
            c_prev(0).wait_recv()
            when(both_ul, r_diag.start)
            when(has_left, r_left.start)

        @pl.when(jnp.logical_and(later, k == 1))
        def _():
            c_prev(1).wait_recv()
            when(has_up, r_up.start)

        return carry

    lax.fori_loop(0, steps, first_pair, 0)

    @pl.when(later)
    def _():
        c_prev(2).wait_recv()
        when(has_right, r_left.wait_recv)
        when(has_down, r_up.wait_recv)
        when(both_dr, r_diag.wait_recv)
        for f in range(2):
            for k in range(n_left):
                assemble(f, k * ROWS)
            assemble_low(f)

    early = [jnp.where(is_first, 2, f) for f in range(2)]

    def prev_acts(k, carry):
        for f in range(2):
            activate(tile, early[f], f, k * ROWS, norm)
        return carry

    lax.fori_loop(0, steps, prev_acts, 0)
    close_top(0, 2)
    close_bottom(0, 2)
    keep_hidden(0, 0, side, steps)

    slot_rows = [ROWS] * steps + [side]
    slot_of = [2 * rows * side // 8 for rows in slot_rows]
    center = sum(hid_mean[i] * (n * 8.0 / members) for i, n in enumerate(slot_of))
    center = jnp.mean(center, axis=0, keepdims=True)
    spread = 0.0
    for i, n in enumerate(slot_of):
        off = hid_mean[i] - center
        spread = spread + hid_dev[i] + n * off * off
    spread = jnp.sum(spread, axis=0, keepdims=True)
    stat_tx[...] = rows8((center, spread))
    s_copies = [
        pltpu.make_async_remote_copy(
            src_ref=stat_tx,
            dst_ref=stat_rx.at[j - 1],
            send_sem=stat_send.at[j - 1],
            recv_sem=stat_recv.at[j - 1],
            device_id=dev(0, 0, j),
            device_id_type=MESH,
        )
        for j in range(1, n_span)
    ]
    for c in s_copies:
        c.start()

    @pl.when(has_next)
    def _():
        for i in range(steps // 2, steps):
            hid_copy(i).start()

    for c in s_copies:
        c.wait_recv()
    pieces = [(members, center, spread)]
    for j in range(n_span - 1):
        pieces.append((members, stat_rx[j, 0:1], stat_rx[j, 1:2]))
    _, mean, dev2 = merge(pieces)
    norm = coefficients(mean, dev2, gain2, bias2)

    def own_acts(i, c):
        for f in range(2, 2 + frames):
            activate(hid, f, f, i * ROWS, norm)
        return c

    lax.fori_loop(0, steps, own_acts, 0)
    close_top(2, 2 + frames)
    close_bottom(2, 2 + frames)
    for c in w_copies[6:]:
        c.wait()

    def edge_copies(first):
        p = first // 2
        two = pl.ds(first, 2)
        return (
            remote(send_d.at[two], recv_d.at[two], DOWN + p, 1, 0, 0),
            remote(send_c.at[two], recv_c.at[two], CORNER + p, 1, 1, 0),
            remote(send_r.at[two], recv_r.at[two], RIGHT + p, 0, 1, 0),
        )

    def decoded(first, r, rows, c, cols):
        parts = conv_block(wp2, first, r, rows, c, cols)
        return [
            (first + o, part + tile[first + o + 2, r : r + rows, c : c + cols].astype(F32))
            for o, part in enumerate(parts)
        ]

    def edges(first):
        d_copy, c_copy, r_copy = edge_copies(first)
        for f, part in decoded(first, 0, side, stride, OV):
            send_r[f] = part[0:stride].astype(BF16)
            send_c[f] = part[stride:side].astype(BF16)
        when(both_dr, c_copy.start)
        when(has_right, r_copy.start)
        for f, part in decoded(first, stride, OV, 0, stride):
            send_d[f] = part.astype(BF16)
        when(has_down, d_copy.start)

    def interior(first):
        for f, part in decoded(first, 0, stride, 0, stride):
            out[f] = part.astype(BF16)

    ramp = lax.broadcasted_iota(jnp.int32, (1, OV, 1), 1).astype(F32) * (1.0 / OV)

    def blend(first):
        d_copy, c_copy, r_copy = edge_copies(first)
        when(has_up, d_copy.wait_recv)
        when(both_ul, c_copy.wait_recv)

        @pl.when(has_up)
        def _():
            for f in (first, first + 1):
                for i in range(OV):
                    t = i / OV
                    mix = recv_d[f, i].astype(F32) * (1.0 - t) + out[f, i].astype(F32) * t
                    out[f, i] = mix.astype(BF16)

        when(has_left, r_copy.wait_recv)

        @pl.when(both_ul)
        def _():
            for f in (first, first + 1):
                for i in range(OV):
                    t = i / OV
                    mix = recv_c[f, i].astype(F32) * (1.0 - t) + recv_r[f, i].astype(F32) * t
                    recv_r[f, i] = mix.astype(BF16)

        @pl.when(has_left)
        def _():
            for f in (first, first + 1):
                for r in range(0, stride, 8):
                    rows = slice(r, r + 8)
                    here = out[f, rows].astype(F32)
                    mix = recv_r[f, rows].astype(F32) * (1.0 - ramp) + here[:, 0:OV] * ramp
                    out[f, rows] = jnp.concatenate([mix, here[:, OV:]], axis=1).astype(BF16)

    edges(last)

    @pl.when(later)
    def _():
        for i in range(steps):
            hid_copy(i).wait_recv()

    def hid_acts(i, carry):
        for f in range(2):
            activate(hid, early[f], f, i * ROWS, norm)
        return carry

    lax.fori_loop(0, steps, hid_acts, 0)
    close_top(0, 2)
    close_bottom(0, 2)
    edges(0)
    interior(last)
    interior(0)
    blend(last)
    blend(0)

    for cond, c in sent:
        maybe(cond, c.wait_send)
    when(has_up, c_up.wait_send)
    when(can_lift, c_lift.wait_send)

    @pl.when(has_left)
    def _():
        for i in range(n_left):
            c_left(i).wait_send()

    @pl.when(has_next)
    def _():
        for i in range(3):
            c_prev(i).wait_send()
        for i in range(steps):
            hid_copy(i).wait_send()

    @pl.when(later)
    def _():
        when(has_up, r_up.wait_send)
        when(both_ul, r_diag.wait_send)
        when(has_left, r_left.wait_send)

    for c in s_copies:
        c.wait_send()
    for first in (0, last):
        d_copy, c_copy, r_copy = edge_copies(first)
        when(has_down, d_copy.wait_send)
        when(both_dr, c_copy.wait_send)
        when(has_right, r_copy.wait_send)


def body(sizes, features, norm1_gain, norm1_bias, conv1_weight, norm2_gain, norm2_bias, conv2_weight):
    frames, stride, _, chan = features.shape
    side = stride + OV
    n_other = max(sizes[2] - 1, 1)
    vmem = pl.BlockSpec(memory_space=pltpu.VMEM)
    hbm = pl.BlockSpec(memory_space=pltpu.HBM)
    flat = lambda v: v.reshape(1, chan)
    taps = lambda w: w.reshape(3, 3, 3 * chan, chan)
    flops = 2 * 2 * frames * side * side * 27 * chan * chan
    result = pl.pallas_call(
        functools.partial(kernel, sizes),
        out_shape=pltpu.VMEM(features.shape, BF16),
        in_specs=[hbm] * 7,
        out_specs=vmem,
        scratch_shapes=[
            pltpu.VMEM((frames + 2, stride, stride, chan), BF16),
            pltpu.VMEM((frames + 2, OV, stride, chan), BF16),
            pltpu.VMEM((frames + 2, stride, OV, chan), BF16),
            pltpu.VMEM((frames + 2, OV, OV, chan), BF16),
            pltpu.VMEM((frames + 2, side, side, chan), BF16),
            pltpu.VMEM((side + 2, side, (frames + 2) * 3 * chan), BF16),
            pltpu.VMEM((frames + 2, side, side, chan), BF16),
            pltpu.VMEM((3, 12 * chan, 2 * chan), BF16),
            pltpu.VMEM((3, 12 * chan, 2 * chan), BF16),
            pltpu.VMEM((frames, OV, stride, chan), BF16),
            pltpu.VMEM((frames, stride, OV, chan), BF16),
            pltpu.VMEM((frames, OV, OV, chan), BF16),
            pltpu.VMEM((frames, OV, stride, chan), BF16),
            pltpu.VMEM((frames, stride, OV, chan), BF16),
            pltpu.VMEM((frames, OV, OV, chan), BF16),
            pltpu.VMEM((side // ROWS + 1, 8, chan), F32),
            pltpu.VMEM((side // ROWS + 1, 8, chan), F32),
            pltpu.VMEM((4, 8, chan), F32),
            pltpu.VMEM((sizes[2], 4, 8, chan), F32),
            pltpu.VMEM((8, chan), F32),
            pltpu.VMEM((n_other, 8, chan), F32),
            pltpu.SemaphoreType.DMA((N_SEM,)),
            pltpu.SemaphoreType.DMA((N_SEM,)),
            pltpu.SemaphoreType.DMA((sizes[2], 4)),
            pltpu.SemaphoreType.DMA((sizes[2], 4)),
            pltpu.SemaphoreType.DMA((n_other,)),
            pltpu.SemaphoreType.DMA((n_other,)),
            pltpu.SemaphoreType.DMA((12,)),
            pltpu.SemaphoreType.DMA,
            *[pltpu.VMEM((1, chan), F32) for _ in range(4)],
            pltpu.SemaphoreType.DMA((4,)),
        ],
        compiler_params=pltpu.CompilerParams(
            collective_id=0, has_side_effects=True, vmem_limit_bytes=40_000_000
        ),
        cost_estimate=pl.CostEstimate(
            flops=flops, bytes_accessed=4 << 20, transcendentals=12 * side * side * chan
        ),
    )(
        *[
            pltpu.with_memory_space_constraint(v, pltpu.HBM)
            for v in (
                features,
                flat(norm1_gain),
                flat(norm1_bias),
                taps(conv1_weight),
                flat(norm2_gain),
                flat(norm2_bias),
                taps(conv2_weight),
            )
        ]
    )
    return result


def solution(mesh):
    sizes = tuple(mesh.shape[a] for a in ("trow", "tcol", "span"))
    placed = (P("span", "trow", "tcol", None), P(), P(), P(), P(), P(), P())
    return jax.shard_map(
        functools.partial(body, sizes),
        mesh=mesh,
        in_specs=placed,
        out_specs=P("span", "trow", "tcol", None),
        check_vma=False,
    )
```

```python
import functools

import jax
import jax.numpy as jnp
from jax import lax
from jax.experimental import pallas as pl
from jax.experimental.pallas import tpu as pltpu
from jax.sharding import PartitionSpec as P

G = 32
OV = 8
EPSILON = 1e-06
F32 = jnp.float32
BF16 = jnp.bfloat16
MESH = pl.DeviceIdType.MESH
ROWS = 8

UP, LIFT, LEFT = 0, 1, 2
PREV, R_UP, R_DIAG, R_LEFT = 5, 8, 9, 10
HID = 11
DOWN, CORNER, RIGHT = 15, 17, 19
N_SEM = 21
FULL, TOP, SIDE, BOTH = range(4)


def group_sum(x, size):
    lane = lax.broadcasted_iota(jnp.int32, x.shape, 1)
    width = x.shape[1]
    step = 1
    while step < size:
        low = (lane // step) % 2 == 0
        x = x + jnp.where(low, pltpu.roll(x, width - step, 1), pltpu.roll(x, step, 1))
        step *= 2
    return x


def kernel(
    sizes,
    feat,
    gain1_hbm,
    bias1_hbm,
    w1,
    gain2_hbm,
    bias2_hbm,
    w2,
    out,
    own,
    halo_b,
    halo_r,
    halo_c,
    tile,
    acts,
    hid,
    wp1,
    wp2,
    send_d,
    send_r,
    send_c,
    recv_d,
    recv_r,
    recv_c,
    hid_mean,
    hid_dev,
    piece_tx,
    piece_rx,
    stat_tx,
    stat_rx,
    send_sem,
    recv_sem,
    piece_send,
    piece_recv,
    stat_send,
    stat_recv,
    w_sem,
    own_sem,
    gain1,
    bias1,
    gain2,
    bias2,
    param_sem,
):
    n_row, n_col, n_span = sizes
    frames, stride, _, chan = feat.shape
    side = stride + OV
    steps = side // ROWS
    group = chan // G
    row, col, span = (lax.axis_index(a) for a in ("trow", "tcol", "span"))
    has_up, has_down = row > 0, row < n_row - 1
    has_left, has_right = col > 0, col < n_col - 1
    both_ul = jnp.logical_and(has_up, has_left)
    both_dr = jnp.logical_and(has_down, has_right)
    is_first, later, has_next = span == 0, span > 0, span < n_span - 1

    def dev(dr, dc, ds):
        return {
            "trow": lax.rem(row + dr + n_row, n_row),
            "tcol": lax.rem(col + dc + n_col, n_col),
            "span": lax.rem(span + ds + n_span, n_span),
        }

    def remote(src, dst, k, dr, dc, ds):
        return pltpu.make_async_remote_copy(
            src_ref=src,
            dst_ref=dst,
            send_sem=send_sem.at[k],
            recv_sem=recv_sem.at[k],
            device_id=dev(dr, dc, ds),
            device_id_type=MESH,
        )

    def when(cond, fn):
        @pl.when(cond)
        def _():
            fn()

    own_copy = pltpu.make_async_copy(feat, own.at[2 : 2 + frames], own_sem)
    own_copy.start()
    barrier = pltpu.get_barrier_semaphore()
    near = [
        (has_up, -1, 0),
        (has_down, 1, 0),
        (has_left, 0, -1),
        (has_right, 0, 1),
        (both_ul, -1, -1),
        (both_dr, 1, 1),
    ]

    def greet(dr, dc, ds):
        pl.semaphore_signal(barrier, inc=1, device_id=dev(dr, dc, ds), device_id_type=MESH)

    count = jnp.asarray(n_span - 1, jnp.int32)
    for cond, dr, dc in near:

        @pl.when(cond)
        def _():
            for j in range(n_span):
                greet(dr, dc, j)

        count = count + cond.astype(jnp.int32) * n_span
    for j in range(1, n_span):
        greet(0, 0, j)

    members = frames * side * side

    def rows8(parts):
        parts = list(parts)
        pad = jnp.zeros((8 - len(parts), chan), F32)
        return jnp.concatenate(parts + [pad], axis=0)

    def merge(pieces):
        n = sum(p[0] for p in pieces)
        mean = sum(p[1] * (p[0] / n) for p in pieces)
        dev = sum(p[2] + p[0] * (p[1] - mean) * (p[1] - mean) for p in pieces)
        return n, mean, dev

    def quarters(f):
        x = own[f].astype(F32)
        return (
            x[0:OV, 0:OV],
            x[0:OV, OV:stride],
            x[OV:stride, 0:OV],
            x[OV:stride, OV:stride],
        )

    def fold8(x):
        return jnp.sum(x.reshape(-1, 8, chan), axis=0)

    inner = stride - OV
    counts = [frames * a for a in (OV * OV, OV * inner, inner * OV, inner * inner)]
    none = tuple(jnp.zeros((8, chan), F32) for _ in range(4))
    own_copy.wait()
    sums = lax.fori_loop(
        2, 2 + frames, lambda f, t: tuple(a + fold8(q) for a, q in zip(t, quarters(f))), none
    )
    means = [jnp.sum(t, axis=0, keepdims=True) * (1.0 / n) for t, n in zip(sums, counts)]

    def deviations(f, t):
        result = []
        for i, q in enumerate(quarters(f)):
            off = q - means[i][None]
            result.append(t[i] + fold8(off * off))
        return tuple(result)

    devs = lax.fori_loop(2, 2 + frames, deviations, none)
    devs = [jnp.sum(t, axis=0, keepdims=True) for t in devs]
    quads = list(zip(counts, means, devs))
    mine = [merge(quads), merge(quads[0:2]), merge([quads[0], quads[2]]), quads[0]]
    for k, piece in enumerate(mine):
        piece_tx[k] = rows8(piece[1:])

    sent, arrives = [], []
    for j in range(n_span):
        for k, goes, comes, dr, dc in (
            (FULL, None, None, 0, 0),
            (TOP, has_up, has_down, -1, 0),
            (SIDE, has_left, has_right, 0, -1),
            (BOTH, both_ul, both_dr, -1, -1),
        ):
            if j == 0 and k == FULL:
                continue
            c = pltpu.make_async_remote_copy(
                src_ref=piece_tx.at[k],
                dst_ref=piece_rx.at[j, k],
                send_sem=piece_send.at[j, k],
                recv_sem=piece_recv.at[j, k],
                device_id=dev(dr, dc, j),
                device_id_type=MESH,
            )
            sent.append((goes, c))
            arrives.append((comes, c))

    def maybe(cond, fn):
        if cond is None:
            fn()
        else:
            when(cond, fn)

    pl.semaphore_wait(barrier, count)
    for cond, c in sent:
        maybe(cond, c.start)

    mid = slice(2, 2 + frames)
    c_up = remote(feat.at[:, 0:OV], halo_b.at[mid], UP, -1, 0, 0)
    c_lift = remote(halo_r.at[mid, 0:OV], halo_c.at[mid], LIFT, -1, 0, 0)

    def c_left(i):
        rows = pl.ds(i * ROWS, ROWS)
        return remote(feat.at[:, rows, 0:OV], halo_r.at[mid, rows], LEFT + i, 0, -1, 0)

    n_left = stride // ROWS

    def c_prev(i):
        rows, cols = (
            (slice(0, stride), slice(0, OV)),
            (slice(0, OV), slice(OV, stride)),
            (slice(OV, stride), slice(OV, stride)),
        )[i]
        src = feat.at[frames - 2 : frames, rows, cols]
        return remote(src, own.at[0:2, rows, cols], PREV + i, 0, 0, 1)

    r_up = remote(own.at[0:2, 0:OV], halo_b.at[0:2], R_UP, -1, 0, 0)
    r_diag = remote(own.at[0:2, 0:OV, 0:OV], halo_c.at[0:2], R_DIAG, -1, -1, 0)
    r_left = remote(own.at[0:2, :, 0:OV], halo_r.at[0:2], R_LEFT, 0, -1, 0)

    @pl.when(has_next)
    def _():
        for i in range(3):
            c_prev(i).start()

    @pl.when(has_left)
    def _():
        for i in range(n_left):
            c_left(i).start()

    when(has_up, c_up.start)
    p_copies = [
        pltpu.make_async_copy(src, dst, param_sem.at[k])
        for k, (src, dst) in enumerate(
            ((gain1_hbm, gain1), (bias1_hbm, bias1), (gain2_hbm, gain2), (bias2_hbm, bias2))
        )
    ]
    for c in p_copies:
        c.start()
    w_copies = []
    for n, (w, wp) in enumerate(((w1, wp1), (w2, wp2))):
        for kt in range(3):
            for o in range(2):
                k = (kt + o) * 3 * chan
                w_copies.append(
                    pltpu.make_async_copy(
                        w.at[kt],
                        wp.at[:, k : k + 3 * chan, o * chan : (o + 1) * chan],
                        w_sem.at[n * 6 + kt * 2 + o],
                    )
                )
    for c in w_copies:
        c.start()

    def zero(ref):
        ref[...] = jnp.zeros(ref.shape, ref.dtype)

    when(jnp.logical_not(has_down), lambda: zero(halo_b))
    when(jnp.logical_not(has_right), lambda: zero(halo_r))
    when(jnp.logical_not(both_dr), lambda: zero(halo_c))
    for j in range(n_span):
        when(jnp.logical_not(has_down), lambda: zero(piece_rx.at[j, TOP]))
        when(jnp.logical_not(has_right), lambda: zero(piece_rx.at[j, SIDE]))
        when(jnp.logical_not(both_dr), lambda: zero(piece_rx.at[j, BOTH]))
    for wp in (wp1, wp2):
        wp[:, 0 : 3 * chan, chan:] = jnp.zeros((3, 3 * chan, chan), BF16)
        wp[:, 9 * chan : 12 * chan, 0:chan] = jnp.zeros((3, 3 * chan, chan), BF16)

    def assemble(f, r):
        rows = pl.ds(r, ROWS)
        part = jnp.concatenate([own[f, rows].astype(F32), halo_r[f, rows].astype(F32)], axis=1)
        tile[f, rows] = part.astype(BF16)

    def assemble_low(f):
        part = jnp.concatenate([halo_b[f].astype(F32), halo_c[f].astype(F32)], axis=1)
        tile[f, stride:side] = part.astype(BF16)

    def coefficients(mean, dev2, gain, bias):
        wide = lambda v: jnp.broadcast_to(v, (8, chan))
        center = group_sum(wide(mean), group) * (1.0 / group)
        off = mean - center
        spread = group_sum(wide(dev2) + (members * n_span) * off * off, group)
        inv = lax.rsqrt(spread * (1.0 / (members * group * n_span)) + EPSILON)
        scale = inv[0:1] * (0.5 * gain[...])
        return scale, 0.5 * bias[...] - center[0:1] * scale

    def lanes_of(f):
        return f * 3 * chan if isinstance(f, int) else pl.multiple_of(f * (3 * chan), chan)

    def activate(ref, src, f, r, norm):
        scale, shift = norm
        base = lanes_of(f)
        x = ref[src, pl.ds(r, ROWS)].astype(F32)
        u = x * scale[None] + shift[None]
        y = u * jnp.tanh(u) + u
        left = jnp.concatenate([y[:, 0:1], y[:, 0 : side - 1]], axis=1)
        right = jnp.concatenate([y[:, 1:side], y[:, side - 1 : side]], axis=1)
        rows = pl.ds(r + 1, ROWS)
        for kw, v in enumerate((left, y, right)):
            acts[rows, :, pl.ds(base + kw * chan, chan)] = v.astype(BF16)

    def activate_all(ref, lo, hi, r, norm):
        for f in range(lo, hi):
            activate(ref, f, f, r, norm)

    def close_top(lo, hi):
        lanes = slice(lo * 3 * chan, hi * 3 * chan)
        acts[0, :, lanes] = acts[1, :, lanes]

    def close_bottom(lo, hi):
        lanes = slice(lo * 3 * chan, hi * 3 * chan)
        acts[side + 1, :, lanes] = acts[side, :, lanes]

    def conv_block(wp, first, r, rows, c, cols):
        base = lanes_of(first)
        acc = None
        for kh in range(3):
            lhs = acts[pl.ds(r + kh, rows), c : c + cols, pl.ds(base, 12 * chan)]
            part = jnp.dot(
                lhs.reshape(rows * cols, 12 * chan), wp[kh], preferred_element_type=F32
            )
            acc = part if acc is None else acc + part
        return [acc[:, o * chan : (o + 1) * chan].reshape(rows, cols, chan) for o in range(2)]

    def hid_copy(i):
        rows = pl.ds(i * ROWS, ROWS)
        return remote(hid.at[frames : frames + 2, rows], hid.at[0:2, rows], HID + i, 0, 0, 1)

    def keep_hidden(first, r, rows, slot):
        parts = [p.astype(BF16) for p in conv_block(wp1, first, r, rows, 0, side)]
        wide = []
        for o, part in enumerate(parts):
            hid[first + 2 + o, pl.ds(r, rows)] = part
            wide.append(part.astype(F32))
        center = (fold8(wide[0]) + fold8(wide[1])) * (8.0 / (2 * rows * side))
        off = [(w.reshape(-1, 8, chan) - center[None]) for w in wide]
        hid_mean[slot] = center
        hid_dev[slot] = fold8(off[0] * off[0]) + fold8(off[1] * off[1])

    for c in p_copies:
        c.wait()
    for cond, c in arrives:
        maybe(cond, c.wait_recv)
    area = [frames * a for a in (stride * stride, OV * stride, stride * OV, OV * OV)]
    pieces = [mine[FULL]]
    for j in range(n_span):
        for k in range(4):
            if j or k:
                pieces.append((area[k], piece_rx[j, k, 0:1], piece_rx[j, k, 1:2]))
    _, mean, dev2 = merge(pieces)
    norm = coefficients(mean, dev2, gain1, bias1)

    middle = range(2, 2 + frames)
    can_lift = jnp.logical_and(has_up, has_right)
    when(has_right, c_left(0).wait_recv)
    when(can_lift, c_lift.start)
    for f in middle:
        assemble(f, 0)
    activate_all(tile, 2, 2 + frames, 0, norm)
    close_top(2, 2 + frames)
    for c in w_copies[:6]:
        c.wait()

    last = frames - 2

    def first_pair(k, carry):
        n = k + 1

        @pl.when(n < n_left)
        def _():
            when(has_right, c_left(n).wait_recv)
            for f in middle:
                assemble(f, n * ROWS)

        @pl.when(n == n_left)
        def _():
            when(has_down, c_up.wait_recv)
            when(both_dr, c_lift.wait_recv)
            for f in middle:
                assemble_low(f)

        when(n < steps, lambda: activate_all(tile, 2, 2 + frames, n * ROWS, norm))

        when(n == n_left, lambda: close_bottom(2, 2 + frames))
        keep_hidden(last, k * ROWS, ROWS, k)
        when(jnp.logical_and(has_next, k < steps // 2), hid_copy(k).start)

        @pl.when(jnp.logical_and(later, k == 0))
        def _():
            c_prev(0).wait_recv()
            when(both_ul, r_diag.start)
            when(has_left, r_left.start)

        @pl.when(jnp.logical_and(later, k == 1))
        def _():
            c_prev(1).wait_recv()
            when(has_up, r_up.start)

        return carry

    lax.fori_loop(0, steps, first_pair, 0)

    @pl.when(later)
    def _():
        c_prev(2).wait_recv()
        when(has_right, r_left.wait_recv)
        when(has_down, r_up.wait_recv)
        when(both_dr, r_diag.wait_recv)
        for f in range(2):
            for k in range(n_left):
                assemble(f, k * ROWS)
            assemble_low(f)

    def activate_early(ref, norm):
        def step(i, carry):
            for f in range(2):
                activate(ref, jnp.where(is_first, 2, f), f, i * ROWS, norm)
            return carry

        lax.fori_loop(0, steps, step, 0)
        close_top(0, 2)
        close_bottom(0, 2)

    activate_early(tile, norm)

    def second_pair(k, carry):
        keep_hidden(0, k * 16, 16, steps + k)
        return carry

    lax.fori_loop(0, side // 16, second_pair, 0)

    slot_rows = [ROWS] * steps + [16] * (side // 16)
    slot_of = [2 * rows * side // 8 for rows in slot_rows]
    center = sum(hid_mean[i] * (n * 8.0 / members) for i, n in enumerate(slot_of))
    center = jnp.mean(center, axis=0, keepdims=True)
    spread = 0.0
    for i, n in enumerate(slot_of):
        off = hid_mean[i] - center
        spread = spread + hid_dev[i] + n * off * off
    spread = jnp.sum(spread, axis=0, keepdims=True)
    stat_tx[...] = rows8((center, spread))
    s_copies = [
        pltpu.make_async_remote_copy(
            src_ref=stat_tx,
            dst_ref=stat_rx.at[j - 1],
            send_sem=stat_send.at[j - 1],
            recv_sem=stat_recv.at[j - 1],
            device_id=dev(0, 0, j),
            device_id_type=MESH,
        )
        for j in range(1, n_span)
    ]
    for c in s_copies:
        c.start()

    @pl.when(has_next)
    def _():
        for i in range(steps // 2, steps):
            hid_copy(i).start()

    for c in s_copies:
        c.wait_recv()
    pieces = [(members, center, spread)]
    for j in range(n_span - 1):
        pieces.append((members, stat_rx[j, 0:1], stat_rx[j, 1:2]))
    _, mean, dev2 = merge(pieces)
    norm = coefficients(mean, dev2, gain2, bias2)

    def own_acts(i, c):
        activate_all(hid, 2, 2 + frames, i * ROWS, norm)
        return c

    lax.fori_loop(0, steps, own_acts, 0)
    close_top(2, 2 + frames)
    close_bottom(2, 2 + frames)
    for c in w_copies[6:]:
        c.wait()

    def edge_copies(p):
        first = last * (1 - p)
        two = pl.ds(first, 2)
        return (
            remote(send_d.at[two], recv_d.at[two], DOWN + p, 1, 0, 0),
            remote(send_c.at[two], recv_c.at[two], CORNER + p, 1, 1, 0),
            remote(send_r.at[two], recv_r.at[two], RIGHT + p, 0, 1, 0),
        )

    def decoded(first, r, rows, c, cols):
        parts = conv_block(wp2, first, r, rows, c, cols)
        at = pl.ds(r, rows)
        return [
            (first + o, part + tile[first + o + 2, at, c : c + cols].astype(F32))
            for o, part in enumerate(parts)
        ]

    def decoded_edges(first):
        base = lanes_of(first)
        acc = None
        for kh in range(3):
            lanes = pl.ds(base, 12 * chan)
            tall = acts[kh : kh + side, stride:side, lanes].reshape(side * OV, 12 * chan)
            low = acts[stride + kh : side + kh, 0:stride, lanes].reshape(stride * OV, 12 * chan)
            lhs = jnp.concatenate([tall, low], axis=0)
            part = jnp.dot(lhs, wp2[kh], preferred_element_type=F32)
            acc = part if acc is None else acc + part
        result = []
        for o in range(2):
            f = first + o
            mine = acc[:, o * chan : (o + 1) * chan]
            tall = mine[0 : side * OV].reshape(side, OV, chan)
            low = mine[side * OV :].reshape(OV, stride, chan)
            tall = tall + tile[f + 2, :, stride:side].astype(F32)
            low = low + tile[f + 2, stride:side, 0:stride].astype(F32)
            result.append((f, tall, low))
        return result

    def edges(p, carry):
        first = last * (1 - p)

        @pl.when(p == 1)
        def _():
            @pl.when(later)
            def _():
                for i in range(steps):
                    hid_copy(i).wait_recv()

            activate_early(hid, norm)

        d_copy, c_copy, r_copy = edge_copies(p)
        for f, tall, low in decoded_edges(first):
            send_r[f] = tall[0:stride].astype(BF16)
            send_c[f] = tall[stride:side].astype(BF16)
            send_d[f] = low.astype(BF16)
        when(both_dr, c_copy.start)
        when(has_right, r_copy.start)
        when(has_down, d_copy.start)
        return carry

    parts = stride // 24

    def interior(i, carry):
        first = last * (1 - lax.div(i, parts))
        r = lax.rem(i, parts) * 24
        for f, part in decoded(first, r, 24, 0, stride):
            out[f, pl.ds(r, 24)] = part.astype(BF16)
        return carry

    def interior_at(i):
        first = last * (1 - i)
        for f, part in decoded(first, 0, stride, 0, stride):
            out[f] = part.astype(BF16)

    ramp = lax.broadcasted_iota(jnp.int32, (1, OV, 1), 1).astype(F32) * (1.0 / OV)

    def blend(p):
        first = last * (1 - p)
        d_copy, c_copy, r_copy = edge_copies(p)
        when(has_up, d_copy.wait_recv)
        when(both_ul, c_copy.wait_recv)

        @pl.when(has_up)
        def _():
            for f in (first, first + 1):
                for i in range(OV):
                    t = i / OV
                    mix = recv_d[f, i].astype(F32) * (1.0 - t) + out[f, i].astype(F32) * t
                    out[f, i] = mix.astype(BF16)

        when(has_left, r_copy.wait_recv)

        @pl.when(both_ul)
        def _():
            for f in (first, first + 1):
                for i in range(OV):
                    t = i / OV
                    mix = recv_c[f, i].astype(F32) * (1.0 - t) + recv_r[f, i].astype(F32) * t
                    recv_r[f, i] = mix.astype(BF16)

        @pl.when(has_left)
        def _():
            for f in (first, first + 1):
                for r in range(0, stride, 8):
                    rows = slice(r, r + 8)
                    here = out[f, rows].astype(F32)
                    mix = recv_r[f, rows].astype(F32) * (1.0 - ramp) + here[:, 0:OV] * ramp
                    out[f, rows] = jnp.concatenate([mix, here[:, OV:]], axis=1).astype(BF16)

    lax.fori_loop(0, 2, edges, 0)
    interior_at(0)
    interior_at(1)
    blend(0)
    blend(1)

    for cond, c in sent:
        maybe(cond, c.wait_send)
    when(has_up, c_up.wait_send)
    when(can_lift, c_lift.wait_send)

    @pl.when(has_left)
    def _():
        for i in range(n_left):
            c_left(i).wait_send()

    @pl.when(has_next)
    def _():
        for i in range(3):
            c_prev(i).wait_send()
        for i in range(steps):
            hid_copy(i).wait_send()

    @pl.when(later)
    def _():
        when(has_up, r_up.wait_send)
        when(both_ul, r_diag.wait_send)
        when(has_left, r_left.wait_send)

    for c in s_copies:
        c.wait_send()
    for p in range(2):
        d_copy, c_copy, r_copy = edge_copies(p)
        when(has_down, d_copy.wait_send)
        when(both_dr, c_copy.wait_send)
        when(has_right, r_copy.wait_send)


def body(sizes, features, norm1_gain, norm1_bias, conv1_weight, norm2_gain, norm2_bias, conv2_weight):
    frames, stride, _, chan = features.shape
    side = stride + OV
    n_other = max(sizes[2] - 1, 1)
    vmem = pl.BlockSpec(memory_space=pltpu.VMEM)
    hbm = pl.BlockSpec(memory_space=pltpu.HBM)
    flat = lambda v: v.reshape(1, chan)
    taps = lambda w: w.reshape(3, 3, 3 * chan, chan)
    flops = 2 * 2 * frames * side * side * 27 * chan * chan
    result = pl.pallas_call(
        functools.partial(kernel, sizes),
        out_shape=pltpu.VMEM(features.shape, BF16),
        in_specs=[hbm] * 7,
        out_specs=vmem,
        scratch_shapes=[
            pltpu.VMEM((frames + 2, stride, stride, chan), BF16),
            pltpu.VMEM((frames + 2, OV, stride, chan), BF16),
            pltpu.VMEM((frames + 2, stride, OV, chan), BF16),
            pltpu.VMEM((frames + 2, OV, OV, chan), BF16),
            pltpu.VMEM((frames + 2, side, side, chan), BF16),
            pltpu.VMEM((side + 2, side, (frames + 2) * 3 * chan), BF16),
            pltpu.VMEM((frames + 2, side, side, chan), BF16),
            pltpu.VMEM((3, 12 * chan, 2 * chan), BF16),
            pltpu.VMEM((3, 12 * chan, 2 * chan), BF16),
            pltpu.VMEM((frames, OV, stride, chan), BF16),
            pltpu.VMEM((frames, stride, OV, chan), BF16),
            pltpu.VMEM((frames, OV, OV, chan), BF16),
            pltpu.VMEM((frames, OV, stride, chan), BF16),
            pltpu.VMEM((frames, stride, OV, chan), BF16),
            pltpu.VMEM((frames, OV, OV, chan), BF16),
            pltpu.VMEM((side // ROWS * 2, 8, chan), F32),
            pltpu.VMEM((side // ROWS * 2, 8, chan), F32),
            pltpu.VMEM((4, 8, chan), F32),
            pltpu.VMEM((sizes[2], 4, 8, chan), F32),
            pltpu.VMEM((8, chan), F32),
            pltpu.VMEM((n_other, 8, chan), F32),
            pltpu.SemaphoreType.DMA((N_SEM,)),
            pltpu.SemaphoreType.DMA((N_SEM,)),
            pltpu.SemaphoreType.DMA((sizes[2], 4)),
            pltpu.SemaphoreType.DMA((sizes[2], 4)),
            pltpu.SemaphoreType.DMA((n_other,)),
            pltpu.SemaphoreType.DMA((n_other,)),
            pltpu.SemaphoreType.DMA((12,)),
            pltpu.SemaphoreType.DMA,
            *[pltpu.VMEM((1, chan), F32) for _ in range(4)],
            pltpu.SemaphoreType.DMA((4,)),
        ],
        compiler_params=pltpu.CompilerParams(
            collective_id=0, has_side_effects=True, vmem_limit_bytes=40_000_000
        ),
        cost_estimate=pl.CostEstimate(
            flops=flops, bytes_accessed=4 << 20, transcendentals=12 * side * side * chan
        ),
    )(
        *[
            pltpu.with_memory_space_constraint(v, pltpu.HBM)
            for v in (
                features,
                flat(norm1_gain),
                flat(norm1_bias),
                taps(conv1_weight),
                flat(norm2_gain),
                flat(norm2_bias),
                taps(conv2_weight),
            )
        ]
    )
    return result


def solution(mesh):
    sizes = tuple(mesh.shape[a] for a in ("trow", "tcol", "span"))
    placed = (P("span", "trow", "tcol", None), P(), P(), P(), P(), P(), P())
    return jax.shard_map(
        functools.partial(body, sizes),
        mesh=mesh,
        in_specs=placed,
        out_specs=P("span", "trow", "tcol", None),
        check_vma=False,
    )
```

```python
import functools

import jax
import jax.numpy as jnp
from jax import lax
from jax.experimental import pallas as pl
from jax.experimental.pallas import tpu as pltpu
from jax.sharding import PartitionSpec as P

G = 32
OV = 8
EPSILON = 1e-06
F32 = jnp.float32
BF16 = jnp.bfloat16
MESH = pl.DeviceIdType.MESH
ROWS = 8

UP, LIFT, LEFT = 0, 1, 2
PREV, R_UP, R_DIAG, R_LEFT = 5, 8, 9, 10
HID = 11
DOWN, CORNER, RIGHT = 15, 17, 19
N_SEM = 21
FULL, TOP, SIDE, BOTH = range(4)


def group_sum(x, size):
    lane = lax.broadcasted_iota(jnp.int32, x.shape, 1)
    width = x.shape[1]
    step = 1
    while step < size:
        low = (lane // step) % 2 == 0
        x = x + jnp.where(low, pltpu.roll(x, width - step, 1), pltpu.roll(x, step, 1))
        step *= 2
    return x


def kernel(
    sizes,
    feat,
    gain1_hbm,
    bias1_hbm,
    w1,
    gain2_hbm,
    bias2_hbm,
    w2,
    out,
    own,
    halo_b,
    halo_r,
    halo_c,
    tile,
    acts,
    hid,
    wp1,
    wp2,
    send_d,
    send_r,
    send_c,
    recv_d,
    recv_r,
    recv_c,
    hid_mean,
    hid_dev,
    piece_tx,
    piece_rx,
    stat_tx,
    stat_rx,
    send_sem,
    recv_sem,
    piece_send,
    piece_recv,
    stat_send,
    stat_recv,
    w_sem,
    own_sem,
    gain1,
    bias1,
    gain2,
    bias2,
    param_sem,
):
    n_row, n_col, n_span = sizes
    frames, stride, _, chan = feat.shape
    side = stride + OV
    steps = side // ROWS
    group = chan // G
    row, col, span = (lax.axis_index(a) for a in ("trow", "tcol", "span"))
    has_up, has_down = row > 0, row < n_row - 1
    has_left, has_right = col > 0, col < n_col - 1
    both_ul = jnp.logical_and(has_up, has_left)
    both_dr = jnp.logical_and(has_down, has_right)
    is_first, later, has_next = span == 0, span > 0, span < n_span - 1

    def dev(dr, dc, ds):
        return {
            "trow": lax.rem(row + dr + n_row, n_row),
            "tcol": lax.rem(col + dc + n_col, n_col),
            "span": lax.rem(span + ds + n_span, n_span),
        }

    def remote(src, dst, k, dr, dc, ds):
        return pltpu.make_async_remote_copy(
            src_ref=src,
            dst_ref=dst,
            send_sem=send_sem.at[k],
            recv_sem=recv_sem.at[k],
            device_id=dev(dr, dc, ds),
            device_id_type=MESH,
        )

    def when(cond, fn):
        @pl.when(cond)
        def _():
            fn()

    own_copy = pltpu.make_async_copy(feat, own.at[2 : 2 + frames], own_sem)
    own_copy.start()
    barrier = pltpu.get_barrier_semaphore()
    near = [
        (has_up, -1, 0),
        (has_down, 1, 0),
        (has_left, 0, -1),
        (has_right, 0, 1),
        (both_ul, -1, -1),
        (both_dr, 1, 1),
    ]

    def greet(dr, dc, ds):
        pl.semaphore_signal(barrier, inc=1, device_id=dev(dr, dc, ds), device_id_type=MESH)

    count = jnp.asarray(n_span - 1, jnp.int32)
    for cond, dr, dc in near:

        @pl.when(cond)
        def _():
            for j in range(n_span):
                greet(dr, dc, j)

        count = count + cond.astype(jnp.int32) * n_span
    for j in range(1, n_span):
        greet(0, 0, j)

    members = frames * side * side

    def rows8(parts):
        parts = list(parts)
        pad = jnp.zeros((8 - len(parts), chan), F32)
        return jnp.concatenate(parts + [pad], axis=0)

    def merge(pieces):
        n = sum(p[0] for p in pieces)
        mean = sum(p[1] * (p[0] / n) for p in pieces)
        dev = sum(p[2] + p[0] * (p[1] - mean) * (p[1] - mean) for p in pieces)
        return n, mean, dev

    def quarters(f):
        x = own[f].astype(F32)
        return (
            x[0:OV, 0:OV],
            x[0:OV, OV:stride],
            x[OV:stride, 0:OV],
            x[OV:stride, OV:stride],
        )

    def fold8(x):
        return jnp.sum(x.reshape(-1, 8, chan), axis=0)

    inner = stride - OV
    counts = [frames * a for a in (OV * OV, OV * inner, inner * OV, inner * inner)]
    none = tuple(jnp.zeros((8, chan), F32) for _ in range(4))
    own_copy.wait()
    sums = lax.fori_loop(
        2, 2 + frames, lambda f, t: tuple(a + fold8(q) for a, q in zip(t, quarters(f))), none
    )
    means = [jnp.sum(t, axis=0, keepdims=True) * (1.0 / n) for t, n in zip(sums, counts)]

    def deviations(f, t):
        result = []
        for i, q in enumerate(quarters(f)):
            off = q - means[i][None]
            result.append(t[i] + fold8(off * off))
        return tuple(result)

    devs = lax.fori_loop(2, 2 + frames, deviations, none)
    devs = [jnp.sum(t, axis=0, keepdims=True) for t in devs]
    quads = list(zip(counts, means, devs))
    mine = [merge(quads), merge(quads[0:2]), merge([quads[0], quads[2]]), quads[0]]
    for k, piece in enumerate(mine):
        piece_tx[k] = rows8(piece[1:])

    sent, arrives = [], []
    for j in range(n_span):
        for k, goes, comes, dr, dc in (
            (FULL, None, None, 0, 0),
            (TOP, has_up, has_down, -1, 0),
            (SIDE, has_left, has_right, 0, -1),
            (BOTH, both_ul, both_dr, -1, -1),
        ):
            if j == 0 and k == FULL:
                continue
            c = pltpu.make_async_remote_copy(
                src_ref=piece_tx.at[k],
                dst_ref=piece_rx.at[j, k],
                send_sem=piece_send.at[j, k],
                recv_sem=piece_recv.at[j, k],
                device_id=dev(dr, dc, j),
                device_id_type=MESH,
            )
            sent.append((goes, c))
            arrives.append((comes, c))

    def maybe(cond, fn):
        if cond is None:
            fn()
        else:
            when(cond, fn)

    pl.semaphore_wait(barrier, count)
    for cond, c in sent:
        maybe(cond, c.start)

    mid = slice(2, 2 + frames)
    c_up = remote(feat.at[:, 0:OV], halo_b.at[mid], UP, -1, 0, 0)
    c_lift = remote(halo_r.at[mid, 0:OV], halo_c.at[mid], LIFT, -1, 0, 0)

    def c_left(i):
        rows = pl.ds(i * ROWS, ROWS)
        return remote(feat.at[:, rows, 0:OV], halo_r.at[mid, rows], LEFT + i, 0, -1, 0)

    n_left = stride // ROWS

    def c_prev(i):
        rows, cols = (
            (slice(0, stride), slice(0, OV)),
            (slice(0, OV), slice(OV, stride)),
            (slice(OV, stride), slice(OV, stride)),
        )[i]
        src = feat.at[frames - 2 : frames, rows, cols]
        return remote(src, own.at[0:2, rows, cols], PREV + i, 0, 0, 1)

    r_up = remote(own.at[0:2, 0:OV], halo_b.at[0:2], R_UP, -1, 0, 0)
    r_diag = remote(own.at[0:2, 0:OV, 0:OV], halo_c.at[0:2], R_DIAG, -1, -1, 0)
    r_left = remote(own.at[0:2, :, 0:OV], halo_r.at[0:2], R_LEFT, 0, -1, 0)

    @pl.when(has_next)
    def _():
        for i in range(3):
            c_prev(i).start()

    @pl.when(has_left)
    def _():
        for i in range(n_left):
            c_left(i).start()

    when(has_up, c_up.start)
    p_copies = [
        pltpu.make_async_copy(src, dst, param_sem.at[k])
        for k, (src, dst) in enumerate(
            ((gain1_hbm, gain1), (bias1_hbm, bias1), (gain2_hbm, gain2), (bias2_hbm, bias2))
        )
    ]
    for c in p_copies:
        c.start()
    w_copies = []
    for n, (w, wp) in enumerate(((w1, wp1), (w2, wp2))):
        for kt in range(3):
            for o in range(2):
                k = (kt + o) * 3 * chan
                w_copies.append(
                    pltpu.make_async_copy(
                        w.at[kt],
                        wp.at[:, k : k + 3 * chan, o * chan : (o + 1) * chan],
                        w_sem.at[n * 6 + kt * 2 + o],
                    )
                )
    for c in w_copies:
        c.start()

    def zero(ref):
        ref[...] = jnp.zeros(ref.shape, ref.dtype)

    when(jnp.logical_not(has_down), lambda: zero(halo_b))
    when(jnp.logical_not(has_right), lambda: zero(halo_r))
    when(jnp.logical_not(both_dr), lambda: zero(halo_c))
    for j in range(n_span):
        when(jnp.logical_not(has_down), lambda: zero(piece_rx.at[j, TOP]))
        when(jnp.logical_not(has_right), lambda: zero(piece_rx.at[j, SIDE]))
        when(jnp.logical_not(both_dr), lambda: zero(piece_rx.at[j, BOTH]))
    for wp in (wp1, wp2):
        wp[:, 0 : 3 * chan, chan:] = jnp.zeros((3, 3 * chan, chan), BF16)
        wp[:, 9 * chan : 12 * chan, 0:chan] = jnp.zeros((3, 3 * chan, chan), BF16)

    def assemble(f, r):
        rows = pl.ds(r, ROWS)
        part = jnp.concatenate([own[f, rows].astype(F32), halo_r[f, rows].astype(F32)], axis=1)
        tile[f, rows] = part.astype(BF16)

    def assemble_low(f):
        part = jnp.concatenate([halo_b[f].astype(F32), halo_c[f].astype(F32)], axis=1)
        tile[f, stride:side] = part.astype(BF16)

    def coefficients(mean, dev2, gain, bias):
        wide = lambda v: jnp.broadcast_to(v, (8, chan))
        center = group_sum(wide(mean), group) * (1.0 / group)
        off = mean - center
        spread = group_sum(wide(dev2) + (members * n_span) * off * off, group)
        inv = lax.rsqrt(spread * (1.0 / (members * group * n_span)) + EPSILON)
        scale = inv[0:1] * (0.5 * gain[...])
        return scale, 0.5 * bias[...] - center[0:1] * scale

    def lanes_of(f):
        return f * 3 * chan if isinstance(f, int) else pl.multiple_of(f * (3 * chan), chan)

    def activate(ref, src, f, r, norm):
        scale, shift = norm
        base = lanes_of(f)
        x = ref[src, pl.ds(r, ROWS)].astype(F32)
        u = x * scale[None] + shift[None]
        y = u * jnp.tanh(u) + u
        left = jnp.concatenate([y[:, 0:1], y[:, 0 : side - 1]], axis=1)
        right = jnp.concatenate([y[:, 1:side], y[:, side - 1 : side]], axis=1)
        rows = pl.ds(r + 1, ROWS)
        for kw, v in enumerate((left, y, right)):
            acts[rows, :, pl.ds(base + kw * chan, chan)] = v.astype(BF16)

    def activate_all(ref, lo, hi, r, norm):
        for f in range(lo, hi):
            activate(ref, f, f, r, norm)

    def close_top(lo, hi):
        lanes = slice(lo * 3 * chan, hi * 3 * chan)
        acts[0, :, lanes] = acts[1, :, lanes]

    def close_bottom(lo, hi):
        lanes = slice(lo * 3 * chan, hi * 3 * chan)
        acts[side + 1, :, lanes] = acts[side, :, lanes]

    def conv_block(wp, first, r, rows, c, cols):
        base = lanes_of(first)
        acc = None
        for kh in range(3):
            lhs = acts[pl.ds(r + kh, rows), c : c + cols, pl.ds(base, 12 * chan)]
            part = jnp.dot(
                lhs.reshape(rows * cols, 12 * chan), wp[kh], preferred_element_type=F32
            )
            acc = part if acc is None else acc + part
        return [acc[:, o * chan : (o + 1) * chan].reshape(rows, cols, chan) for o in range(2)]

    def hid_copy(i):
        rows = pl.ds(i * ROWS, ROWS)
        return remote(hid.at[frames : frames + 2, rows], hid.at[0:2, rows], HID + i, 0, 0, 1)

    def keep_hidden(first, r, rows, slot):
        parts = [p.astype(BF16) for p in conv_block(wp1, first, r, rows, 0, side)]
        wide = []
        for o, part in enumerate(parts):
            hid[first + 2 + o, pl.ds(r, rows)] = part
            wide.append(part.astype(F32))
        center = (fold8(wide[0]) + fold8(wide[1])) * (8.0 / (2 * rows * side))
        off = [(w.reshape(-1, 8, chan) - center[None]) for w in wide]
        hid_mean[slot] = center
        hid_dev[slot] = fold8(off[0] * off[0]) + fold8(off[1] * off[1])

    for c in p_copies:
        c.wait()
    for cond, c in arrives:
        maybe(cond, c.wait_recv)
    area = [frames * a for a in (stride * stride, OV * stride, stride * OV, OV * OV)]
    pieces = [mine[FULL]]
    for j in range(n_span):
        for k in range(4):
            if j or k:
                pieces.append((area[k], piece_rx[j, k, 0:1], piece_rx[j, k, 1:2]))
    _, mean, dev2 = merge(pieces)
    norm = coefficients(mean, dev2, gain1, bias1)

    middle = range(2, 2 + frames)
    can_lift = jnp.logical_and(has_up, has_right)
    when(has_right, c_left(0).wait_recv)
    when(can_lift, c_lift.start)
    for f in middle:
        assemble(f, 0)
    activate_all(tile, 2, 2 + frames, 0, norm)
    close_top(2, 2 + frames)
    for c in w_copies[:6]:
        c.wait()

    last = frames - 2

    def first_pair(k, carry):
        n = k + 1

        @pl.when(n < n_left)
        def _():
            when(has_right, c_left(n).wait_recv)
            for f in middle:
                assemble(f, n * ROWS)

        @pl.when(n == n_left)
        def _():
            when(has_down, c_up.wait_recv)
            when(both_dr, c_lift.wait_recv)
            for f in middle:
                assemble_low(f)

        when(n < steps, lambda: activate_all(tile, 2, 2 + frames, n * ROWS, norm))

        when(n == n_left, lambda: close_bottom(2, 2 + frames))
        @pl.when(jnp.logical_and(later, k == 0))
        def _():
            c_prev(0).wait_recv()
            when(both_ul, r_diag.start)
            when(has_left, r_left.start)

        keep_hidden(last, k * ROWS, ROWS, k)
        when(jnp.logical_and(has_next, k < steps // 2), hid_copy(k).start)

        @pl.when(jnp.logical_and(later, k == 0))
        def _():
            c_prev(1).wait_recv()
            when(has_up, r_up.start)

        return carry

    lax.fori_loop(0, steps, first_pair, 0)

    @pl.when(later)
    def _():
        c_prev(2).wait_recv()
        when(has_right, r_left.wait_recv)
        when(has_down, r_up.wait_recv)
        when(both_dr, r_diag.wait_recv)
        for f in range(2):
            for k in range(n_left):
                assemble(f, k * ROWS)
            assemble_low(f)

    def activate_early(ref, norm):
        def step(i, carry):
            for f in range(2):
                activate(ref, jnp.where(is_first, 2, f), f, i * ROWS, norm)
            return carry

        lax.fori_loop(0, steps, step, 0)
        close_top(0, 2)
        close_bottom(0, 2)

    activate_early(tile, norm)

    def second_pair(k, carry):
        keep_hidden(0, k * 16, 16, steps + k)
        return carry

    lax.fori_loop(0, side // 16, second_pair, 0)

    slot_rows = [ROWS] * steps + [16] * (side // 16)
    slot_of = [2 * rows * side // 8 for rows in slot_rows]
    center = sum(hid_mean[i] * (n * 8.0 / members) for i, n in enumerate(slot_of))
    center = jnp.mean(center, axis=0, keepdims=True)
    spread = 0.0
    for i, n in enumerate(slot_of):
        off = hid_mean[i] - center
        spread = spread + hid_dev[i] + n * off * off
    spread = jnp.sum(spread, axis=0, keepdims=True)
    stat_tx[...] = rows8((center, spread))
    s_copies = [
        pltpu.make_async_remote_copy(
            src_ref=stat_tx,
            dst_ref=stat_rx.at[j - 1],
            send_sem=stat_send.at[j - 1],
            recv_sem=stat_recv.at[j - 1],
            device_id=dev(0, 0, j),
            device_id_type=MESH,
        )
        for j in range(1, n_span)
    ]
    for c in s_copies:
        c.start()

    @pl.when(has_next)
    def _():
        for i in range(steps // 2, steps):
            hid_copy(i).start()

    for c in s_copies:
        c.wait_recv()
    pieces = [(members, center, spread)]
    for j in range(n_span - 1):
        pieces.append((members, stat_rx[j, 0:1], stat_rx[j, 1:2]))
    _, mean, dev2 = merge(pieces)
    norm = coefficients(mean, dev2, gain2, bias2)

    def own_acts(i, c):
        activate_all(hid, 2, 2 + frames, i * ROWS, norm)
        return c

    lax.fori_loop(0, steps, own_acts, 0)
    close_top(2, 2 + frames)
    close_bottom(2, 2 + frames)
    for c in w_copies[6:]:
        c.wait()

    def edge_copies(p):
        first = last * (1 - p)
        two = pl.ds(first, 2)
        return (
            remote(send_d.at[two], recv_d.at[two], DOWN + p, 1, 0, 0),
            remote(send_c.at[two], recv_c.at[two], CORNER + p, 1, 1, 0),
            remote(send_r.at[two], recv_r.at[two], RIGHT + p, 0, 1, 0),
        )

    def decoded(first, r, rows, c, cols):
        parts = conv_block(wp2, first, r, rows, c, cols)
        at = pl.ds(r, rows)
        return [
            (first + o, part + tile[first + o + 2, at, c : c + cols].astype(F32))
            for o, part in enumerate(parts)
        ]

    def decoded_edges(first):
        base = lanes_of(first)
        acc = None
        for kh in range(3):
            lanes = pl.ds(base, 12 * chan)
            tall = acts[kh : kh + side, stride:side, lanes].reshape(side * OV, 12 * chan)
            low = acts[stride + kh : side + kh, 0:stride, lanes].reshape(stride * OV, 12 * chan)
            lhs = jnp.concatenate([tall, low], axis=0)
            part = jnp.dot(lhs, wp2[kh], preferred_element_type=F32)
            acc = part if acc is None else acc + part
        result = []
        for o in range(2):
            f = first + o
            mine = acc[:, o * chan : (o + 1) * chan]
            tall = mine[0 : side * OV].reshape(side, OV, chan)
            low = mine[side * OV :].reshape(OV, stride, chan)
            tall = tall + tile[f + 2, :, stride:side].astype(F32)
            low = low + tile[f + 2, stride:side, 0:stride].astype(F32)
            result.append((f, tall, low))
        return result

    def edges(p, carry):
        first = last * (1 - p)

        @pl.when(p == 1)
        def _():
            @pl.when(later)
            def _():
                for i in range(steps):
                    hid_copy(i).wait_recv()

            activate_early(hid, norm)

        d_copy, c_copy, r_copy = edge_copies(p)
        for f, tall, low in decoded_edges(first):
            send_r[f] = tall[0:stride].astype(BF16)
            send_c[f] = tall[stride:side].astype(BF16)
            send_d[f] = low.astype(BF16)
        when(both_dr, c_copy.start)
        when(has_right, r_copy.start)
        when(has_down, d_copy.start)
        return carry

    parts = stride // 24

    def interior(i, carry):
        first = last * (1 - lax.div(i, parts))
        r = lax.rem(i, parts) * 24
        for f, part in decoded(first, r, 24, 0, stride):
            out[f, pl.ds(r, 24)] = part.astype(BF16)
        return carry

    def interior_at(i):
        first = last * (1 - i)
        for f, part in decoded(first, 0, stride, 0, stride):
            out[f] = part.astype(BF16)

    ramp = lax.broadcasted_iota(jnp.int32, (1, OV, 1), 1).astype(F32) * (1.0 / OV)

    def blend(p):
        first = last * (1 - p)
        d_copy, c_copy, r_copy = edge_copies(p)
        when(has_up, d_copy.wait_recv)
        when(both_ul, c_copy.wait_recv)

        @pl.when(has_up)
        def _():
            for f in (first, first + 1):
                for i in range(OV):
                    t = i / OV
                    mix = recv_d[f, i].astype(F32) * (1.0 - t) + out[f, i].astype(F32) * t
                    out[f, i] = mix.astype(BF16)

        when(has_left, r_copy.wait_recv)

        @pl.when(both_ul)
        def _():
            for f in (first, first + 1):
                for i in range(OV):
                    t = i / OV
                    mix = recv_c[f, i].astype(F32) * (1.0 - t) + recv_r[f, i].astype(F32) * t
                    recv_r[f, i] = mix.astype(BF16)

        @pl.when(has_left)
        def _():
            for f in (first, first + 1):
                for r in range(0, stride, 8):
                    rows = slice(r, r + 8)
                    here = out[f, rows].astype(F32)
                    mix = recv_r[f, rows].astype(F32) * (1.0 - ramp) + here[:, 0:OV] * ramp
                    out[f, rows] = jnp.concatenate([mix, here[:, OV:]], axis=1).astype(BF16)

    lax.fori_loop(0, 2, edges, 0)
    interior_at(0)
    interior_at(1)
    blend(0)
    blend(1)

    for cond, c in sent:
        maybe(cond, c.wait_send)
    when(has_up, c_up.wait_send)
    when(can_lift, c_lift.wait_send)

    @pl.when(has_left)
    def _():
        for i in range(n_left):
            c_left(i).wait_send()

    @pl.when(has_next)
    def _():
        for i in range(3):
            c_prev(i).wait_send()
        for i in range(steps):
            hid_copy(i).wait_send()

    @pl.when(later)
    def _():
        when(has_up, r_up.wait_send)
        when(both_ul, r_diag.wait_send)
        when(has_left, r_left.wait_send)

    for c in s_copies:
        c.wait_send()
    for p in range(2):
        d_copy, c_copy, r_copy = edge_copies(p)
        when(has_down, d_copy.wait_send)
        when(both_dr, c_copy.wait_send)
        when(has_right, r_copy.wait_send)


def body(sizes, features, norm1_gain, norm1_bias, conv1_weight, norm2_gain, norm2_bias, conv2_weight):
    frames, stride, _, chan = features.shape
    side = stride + OV
    n_other = max(sizes[2] - 1, 1)
    vmem = pl.BlockSpec(memory_space=pltpu.VMEM)
    hbm = pl.BlockSpec(memory_space=pltpu.HBM)
    flat = lambda v: v.reshape(1, chan)
    taps = lambda w: w.reshape(3, 3, 3 * chan, chan)
    flops = 2 * 2 * frames * side * side * 27 * chan * chan
    result = pl.pallas_call(
        functools.partial(kernel, sizes),
        out_shape=pltpu.VMEM(features.shape, BF16),
        in_specs=[hbm] * 7,
        out_specs=vmem,
        scratch_shapes=[
            pltpu.VMEM((frames + 2, stride, stride, chan), BF16),
            pltpu.VMEM((frames + 2, OV, stride, chan), BF16),
            pltpu.VMEM((frames + 2, stride, OV, chan), BF16),
            pltpu.VMEM((frames + 2, OV, OV, chan), BF16),
            pltpu.VMEM((frames + 2, side, side, chan), BF16),
            pltpu.VMEM((side + 2, side, (frames + 2) * 3 * chan), BF16),
            pltpu.VMEM((frames + 2, side, side, chan), BF16),
            pltpu.VMEM((3, 12 * chan, 2 * chan), BF16),
            pltpu.VMEM((3, 12 * chan, 2 * chan), BF16),
            pltpu.VMEM((frames, OV, stride, chan), BF16),
            pltpu.VMEM((frames, stride, OV, chan), BF16),
            pltpu.VMEM((frames, OV, OV, chan), BF16),
            pltpu.VMEM((frames, OV, stride, chan), BF16),
            pltpu.VMEM((frames, stride, OV, chan), BF16),
            pltpu.VMEM((frames, OV, OV, chan), BF16),
            pltpu.VMEM((side // ROWS * 2, 8, chan), F32),
            pltpu.VMEM((side // ROWS * 2, 8, chan), F32),
            pltpu.VMEM((4, 8, chan), F32),
            pltpu.VMEM((sizes[2], 4, 8, chan), F32),
            pltpu.VMEM((8, chan), F32),
            pltpu.VMEM((n_other, 8, chan), F32),
            pltpu.SemaphoreType.DMA((N_SEM,)),
            pltpu.SemaphoreType.DMA((N_SEM,)),
            pltpu.SemaphoreType.DMA((sizes[2], 4)),
            pltpu.SemaphoreType.DMA((sizes[2], 4)),
            pltpu.SemaphoreType.DMA((n_other,)),
            pltpu.SemaphoreType.DMA((n_other,)),
            pltpu.SemaphoreType.DMA((12,)),
            pltpu.SemaphoreType.DMA,
            *[pltpu.VMEM((1, chan), F32) for _ in range(4)],
            pltpu.SemaphoreType.DMA((4,)),
        ],
        compiler_params=pltpu.CompilerParams(
            collective_id=0, has_side_effects=True, vmem_limit_bytes=40_000_000
        ),
        cost_estimate=pl.CostEstimate(
            flops=flops, bytes_accessed=4 << 20, transcendentals=12 * side * side * chan
        ),
    )(
        *[
            pltpu.with_memory_space_constraint(v, pltpu.HBM)
            for v in (
                features,
                flat(norm1_gain),
                flat(norm1_bias),
                taps(conv1_weight),
                flat(norm2_gain),
                flat(norm2_bias),
                taps(conv2_weight),
            )
        ]
    )
    return result


def solution(mesh):
    sizes = tuple(mesh.shape[a] for a in ("trow", "tcol", "span"))
    placed = (P("span", "trow", "tcol", None), P(), P(), P(), P(), P(), P())
    return jax.shard_map(
        functools.partial(body, sizes),
        mesh=mesh,
        in_specs=placed,
        out_specs=P("span", "trow", "tcol", None),
        check_vma=False,
    )
```

```python
import functools

import jax
import jax.numpy as jnp
from jax import lax
from jax.experimental import pallas as pl
from jax.experimental.pallas import tpu as pltpu
from jax.sharding import PartitionSpec as P

G = 32
OV = 8
EPSILON = 1e-06
F32 = jnp.float32
BF16 = jnp.bfloat16
MESH = pl.DeviceIdType.MESH
ROWS = 8

UP, LIFT, LEFT = 0, 1, 2
PREV, R_UP, R_DIAG, R_LEFT = 5, 8, 9, 10
HID = 11
DOWN, CORNER, RIGHT = 15, 17, 19
N_SEM = 21
FULL, TOP, SIDE, BOTH = range(4)


def group_sum(x, size):
    lane = lax.broadcasted_iota(jnp.int32, x.shape, 1)
    width = x.shape[1]
    step = 1
    while step < size:
        low = (lane // step) % 2 == 0
        x = x + jnp.where(low, pltpu.roll(x, width - step, 1), pltpu.roll(x, step, 1))
        step *= 2
    return x


def kernel(
    sizes,
    feat,
    gain1_hbm,
    bias1_hbm,
    w1,
    gain2_hbm,
    bias2_hbm,
    w2,
    out,
    own,
    halo_b,
    halo_r,
    halo_c,
    tile,
    acts,
    hid,
    wp1,
    wp2,
    send_d,
    send_r,
    send_c,
    recv_d,
    recv_r,
    recv_c,
    hid_mean,
    hid_dev,
    piece_tx,
    piece_rx,
    stat_tx,
    stat_rx,
    send_sem,
    recv_sem,
    piece_send,
    piece_recv,
    stat_send,
    stat_recv,
    w_sem,
    own_sem,
    gain1,
    bias1,
    gain2,
    bias2,
    param_sem,
):
    n_row, n_col, n_span = sizes
    frames, stride, _, chan = feat.shape
    side = stride + OV
    steps = side // ROWS
    group = chan // G
    row, col, span = (lax.axis_index(a) for a in ("trow", "tcol", "span"))
    has_up, has_down = row > 0, row < n_row - 1
    has_left, has_right = col > 0, col < n_col - 1
    both_ul = jnp.logical_and(has_up, has_left)
    both_dr = jnp.logical_and(has_down, has_right)
    is_first, later, has_next = span == 0, span > 0, span < n_span - 1

    def dev(dr, dc, ds):
        return {
            "trow": lax.rem(row + dr + n_row, n_row),
            "tcol": lax.rem(col + dc + n_col, n_col),
            "span": lax.rem(span + ds + n_span, n_span),
        }

    def remote(src, dst, k, dr, dc, ds):
        return pltpu.make_async_remote_copy(
            src_ref=src,
            dst_ref=dst,
            send_sem=send_sem.at[k],
            recv_sem=recv_sem.at[k],
            device_id=dev(dr, dc, ds),
            device_id_type=MESH,
        )

    def when(cond, fn):
        @pl.when(cond)
        def _():
            fn()

    own_copy = pltpu.make_async_copy(feat, own.at[2 : 2 + frames], own_sem)
    own_copy.start()
    barrier = pltpu.get_barrier_semaphore()
    near = [
        (has_up, -1, 0),
        (has_down, 1, 0),
        (has_left, 0, -1),
        (has_right, 0, 1),
        (both_ul, -1, -1),
        (both_dr, 1, 1),
    ]

    def greet(dr, dc, ds):
        pl.semaphore_signal(barrier, inc=1, device_id=dev(dr, dc, ds), device_id_type=MESH)

    count = jnp.asarray(n_span - 1, jnp.int32)
    for cond, dr, dc in near:

        @pl.when(cond)
        def _():
            for j in range(n_span):
                greet(dr, dc, j)

        count = count + cond.astype(jnp.int32) * n_span
    for j in range(1, n_span):
        greet(0, 0, j)

    members = frames * side * side

    def rows8(parts):
        parts = list(parts)
        pad = jnp.zeros((8 - len(parts), chan), F32)
        return jnp.concatenate(parts + [pad], axis=0)

    def merge(pieces):
        n = sum(p[0] for p in pieces)
        mean = sum(p[1] * (p[0] / n) for p in pieces)
        dev = sum(p[2] + p[0] * (p[1] - mean) * (p[1] - mean) for p in pieces)
        return n, mean, dev

    def quarters(f):
        x = own[f].astype(F32)
        return (
            x[0:OV, 0:OV],
            x[0:OV, OV:stride],
            x[OV:stride, 0:OV],
            x[OV:stride, OV:stride],
        )

    def fold8(x):
        return jnp.sum(x.reshape(-1, 8, chan), axis=0)

    inner = stride - OV
    counts = [frames * a for a in (OV * OV, OV * inner, inner * OV, inner * inner)]
    none = tuple(jnp.zeros((8, chan), F32) for _ in range(4))
    own_copy.wait()
    sums = lax.fori_loop(
        2, 2 + frames, lambda f, t: tuple(a + fold8(q) for a, q in zip(t, quarters(f))), none
    )
    means = [jnp.sum(t, axis=0, keepdims=True) * (1.0 / n) for t, n in zip(sums, counts)]

    def deviations(f, t):
        result = []
        for i, q in enumerate(quarters(f)):
            off = q - means[i][None]
            result.append(t[i] + fold8(off * off))
        return tuple(result)

    devs = lax.fori_loop(2, 2 + frames, deviations, none)
    devs = [jnp.sum(t, axis=0, keepdims=True) for t in devs]
    quads = list(zip(counts, means, devs))
    mine = [merge(quads), merge(quads[0:2]), merge([quads[0], quads[2]]), quads[0]]
    for k, piece in enumerate(mine):
        piece_tx[k] = rows8(piece[1:])

    sent, arrives = [], []
    for j in range(n_span):
        for k, goes, comes, dr, dc in (
            (FULL, None, None, 0, 0),
            (TOP, has_up, has_down, -1, 0),
            (SIDE, has_left, has_right, 0, -1),
            (BOTH, both_ul, both_dr, -1, -1),
        ):
            if j == 0 and k == FULL:
                continue
            c = pltpu.make_async_remote_copy(
                src_ref=piece_tx.at[k],
                dst_ref=piece_rx.at[j, k],
                send_sem=piece_send.at[j, k],
                recv_sem=piece_recv.at[j, k],
                device_id=dev(dr, dc, j),
                device_id_type=MESH,
            )
            sent.append((goes, c))
            arrives.append((comes, c))

    def maybe(cond, fn):
        if cond is None:
            fn()
        else:
            when(cond, fn)

    pl.semaphore_wait(barrier, count)
    for cond, c in sent:
        maybe(cond, c.start)

    mid = slice(2, 2 + frames)
    c_up = remote(feat.at[:, 0:OV], halo_b.at[mid], UP, -1, 0, 0)
    c_lift = remote(halo_r.at[mid, 0:OV], halo_c.at[mid], LIFT, -1, 0, 0)

    def c_left(i):
        rows = pl.ds(i * ROWS, ROWS)
        return remote(feat.at[:, rows, 0:OV], halo_r.at[mid, rows], LEFT + i, 0, -1, 0)

    n_left = stride // ROWS

    def c_prev(i):
        rows, cols = (
            (slice(0, stride), slice(0, OV)),
            (slice(0, OV), slice(OV, stride)),
            (slice(OV, stride), slice(OV, stride)),
        )[i]
        src = feat.at[frames - 2 : frames, rows, cols]
        return remote(src, own.at[0:2, rows, cols], PREV + i, 0, 0, 1)

    r_up = remote(own.at[0:2, 0:OV], halo_b.at[0:2], R_UP, -1, 0, 0)
    r_diag = remote(own.at[0:2, 0:OV, 0:OV], halo_c.at[0:2], R_DIAG, -1, -1, 0)
    r_left = remote(own.at[0:2, :, 0:OV], halo_r.at[0:2], R_LEFT, 0, -1, 0)

    @pl.when(has_next)
    def _():
        for i in range(3):
            c_prev(i).start()

    @pl.when(has_left)
    def _():
        for i in range(n_left):
            c_left(i).start()

    when(has_up, c_up.start)
    p_copies = [
        pltpu.make_async_copy(src, dst, param_sem.at[k])
        for k, (src, dst) in enumerate(
            ((gain1_hbm, gain1), (bias1_hbm, bias1), (gain2_hbm, gain2), (bias2_hbm, bias2))
        )
    ]
    for c in p_copies:
        c.start()
    w_copies = []
    for n, (w, wp) in enumerate(((w1, wp1), (w2, wp2))):
        for kt in range(3):
            for o in range(2):
                k = (kt + o) * 3 * chan
                w_copies.append(
                    pltpu.make_async_copy(
                        w.at[kt],
                        wp.at[:, k : k + 3 * chan, o * chan : (o + 1) * chan],
                        w_sem.at[n * 6 + kt * 2 + o],
                    )
                )
    for c in w_copies:
        c.start()

    def zero(ref):
        ref[...] = jnp.zeros(ref.shape, ref.dtype)

    when(jnp.logical_not(has_down), lambda: zero(halo_b))
    when(jnp.logical_not(has_right), lambda: zero(halo_r))
    when(jnp.logical_not(both_dr), lambda: zero(halo_c))
    for j in range(n_span):
        when(jnp.logical_not(has_down), lambda: zero(piece_rx.at[j, TOP]))
        when(jnp.logical_not(has_right), lambda: zero(piece_rx.at[j, SIDE]))
        when(jnp.logical_not(both_dr), lambda: zero(piece_rx.at[j, BOTH]))
    for wp in (wp1, wp2):
        wp[:, 0 : 3 * chan, chan:] = jnp.zeros((3, 3 * chan, chan), BF16)
        wp[:, 9 * chan : 12 * chan, 0:chan] = jnp.zeros((3, 3 * chan, chan), BF16)

    def assemble(f, r):
        rows = pl.ds(r, ROWS)
        part = jnp.concatenate([own[f, rows].astype(F32), halo_r[f, rows].astype(F32)], axis=1)
        tile[f, rows] = part.astype(BF16)

    def assemble_low(f):
        part = jnp.concatenate([halo_b[f].astype(F32), halo_c[f].astype(F32)], axis=1)
        tile[f, stride:side] = part.astype(BF16)

    def coefficients(mean, dev2, gain, bias):
        wide = lambda v: jnp.broadcast_to(v, (8, chan))
        center = group_sum(wide(mean), group) * (1.0 / group)
        off = mean - center
        spread = group_sum(wide(dev2) + (members * n_span) * off * off, group)
        inv = lax.rsqrt(spread * (1.0 / (members * group * n_span)) + EPSILON)
        scale = inv[0:1] * (0.5 * gain[...])
        return scale, 0.5 * bias[...] - center[0:1] * scale

    def lanes_of(f):
        return f * 3 * chan if isinstance(f, int) else pl.multiple_of(f * (3 * chan), chan)

    def activate(ref, src, f, r, norm):
        scale, shift = norm
        base = lanes_of(f)
        x = ref[src, pl.ds(r, ROWS)].astype(F32)
        u = x * scale[None] + shift[None]
        y = u * jnp.tanh(u) + u
        left = jnp.concatenate([y[:, 0:1], y[:, 0 : side - 1]], axis=1)
        right = jnp.concatenate([y[:, 1:side], y[:, side - 1 : side]], axis=1)
        rows = pl.ds(r + 1, ROWS)
        for kw, v in enumerate((left, y, right)):
            acts[rows, :, pl.ds(base + kw * chan, chan)] = v.astype(BF16)

    def activate_all(ref, lo, hi, r, norm):
        for f in range(lo, hi):
            activate(ref, f, f, r, norm)

    def close_top(lo, hi):
        lanes = slice(lo * 3 * chan, hi * 3 * chan)
        acts[0, :, lanes] = acts[1, :, lanes]

    def close_bottom(lo, hi):
        lanes = slice(lo * 3 * chan, hi * 3 * chan)
        acts[side + 1, :, lanes] = acts[side, :, lanes]

    def conv_block(wp, first, r, rows, c, cols):
        base = lanes_of(first)
        acc = None
        for kh in range(3):
            lhs = acts[pl.ds(r + kh, rows), c : c + cols, pl.ds(base, 12 * chan)]
            part = jnp.dot(
                lhs.reshape(rows * cols, 12 * chan), wp[kh], preferred_element_type=F32
            )
            acc = part if acc is None else acc + part
        return [acc[:, o * chan : (o + 1) * chan].reshape(rows, cols, chan) for o in range(2)]

    def hid_copy(i):
        rows = pl.ds(i * ROWS, ROWS)
        return remote(hid.at[frames : frames + 2, rows], hid.at[0:2, rows], HID + i, 0, 0, 1)

    def keep_hidden(first, r, rows, slot):
        parts = [p.astype(BF16) for p in conv_block(wp1, first, r, rows, 0, side)]
        wide = []
        for o, part in enumerate(parts):
            hid[first + 2 + o, pl.ds(r, rows)] = part
            wide.append(part.astype(F32))
        center = (fold8(wide[0]) + fold8(wide[1])) * (8.0 / (2 * rows * side))
        off = [(w.reshape(-1, 8, chan) - center[None]) for w in wide]
        hid_mean[slot] = center
        hid_dev[slot] = fold8(off[0] * off[0]) + fold8(off[1] * off[1])

    for c in p_copies:
        c.wait()
    for cond, c in arrives:
        maybe(cond, c.wait_recv)
    area = [frames * a for a in (stride * stride, OV * stride, stride * OV, OV * OV)]
    pieces = [mine[FULL]]
    for j in range(n_span):
        for k in range(4):
            if j or k:
                pieces.append((area[k], piece_rx[j, k, 0:1], piece_rx[j, k, 1:2]))
    _, mean, dev2 = merge(pieces)
    norm = coefficients(mean, dev2, gain1, bias1)

    middle = range(2, 2 + frames)
    can_lift = jnp.logical_and(has_up, has_right)
    when(has_right, c_left(0).wait_recv)
    when(can_lift, c_lift.start)
    for f in middle:
        assemble(f, 0)
    activate_all(tile, 2, 2 + frames, 0, norm)
    close_top(2, 2 + frames)
    for c in w_copies[:6]:
        c.wait()

    last = frames - 2

    def first_pair(k, carry):
        n = k + 1

        @pl.when(n < n_left)
        def _():
            when(has_right, c_left(n).wait_recv)
            for f in middle:
                assemble(f, n * ROWS)

        @pl.when(n == n_left)
        def _():
            when(has_down, c_up.wait_recv)
            when(both_dr, c_lift.wait_recv)
            for f in middle:
                assemble_low(f)

        when(n < steps, lambda: activate_all(tile, 2, 2 + frames, n * ROWS, norm))

        when(n == n_left, lambda: close_bottom(2, 2 + frames))
        @pl.when(jnp.logical_and(later, k == 0))
        def _():
            c_prev(0).wait_recv()
            when(both_ul, r_diag.start)
            when(has_left, r_left.start)

        @pl.when(jnp.logical_and(later, k == 0))
        def _():
            c_prev(1).wait_recv()
            when(has_up, r_up.start)

        keep_hidden(last, k * ROWS, ROWS, k)
        when(jnp.logical_and(has_next, k < steps // 2), hid_copy(k).start)

        return carry

    lax.fori_loop(0, steps, first_pair, 0)

    @pl.when(later)
    def _():
        c_prev(2).wait_recv()
        when(has_right, r_left.wait_recv)
        when(has_down, r_up.wait_recv)
        when(both_dr, r_diag.wait_recv)
        for f in range(2):
            for k in range(n_left):
                assemble(f, k * ROWS)
            assemble_low(f)

    def activate_early(ref, norm):
        def step(i, carry):
            for f in range(2):
                activate(ref, jnp.where(is_first, 2, f), f, i * ROWS, norm)
            return carry

        lax.fori_loop(0, steps, step, 0)
        close_top(0, 2)
        close_bottom(0, 2)

    activate_early(tile, norm)

    def second_pair(k, carry):
        keep_hidden(0, k * 16, 16, steps + k)
        return carry

    lax.fori_loop(0, side // 16, second_pair, 0)

    slot_rows = [ROWS] * steps + [16] * (side // 16)
    slot_of = [2 * rows * side // 8 for rows in slot_rows]
    center = sum(hid_mean[i] * (n * 8.0 / members) for i, n in enumerate(slot_of))
    center = jnp.mean(center, axis=0, keepdims=True)
    spread = 0.0
    for i, n in enumerate(slot_of):
        off = hid_mean[i] - center
        spread = spread + hid_dev[i] + n * off * off
    spread = jnp.sum(spread, axis=0, keepdims=True)
    stat_tx[...] = rows8((center, spread))
    s_copies = [
        pltpu.make_async_remote_copy(
            src_ref=stat_tx,
            dst_ref=stat_rx.at[j - 1],
            send_sem=stat_send.at[j - 1],
            recv_sem=stat_recv.at[j - 1],
            device_id=dev(0, 0, j),
            device_id_type=MESH,
        )
        for j in range(1, n_span)
    ]
    for c in s_copies:
        c.start()

    @pl.when(has_next)
    def _():
        for i in range(steps // 2, steps):
            hid_copy(i).start()

    for c in s_copies:
        c.wait_recv()
    pieces = [(members, center, spread)]
    for j in range(n_span - 1):
        pieces.append((members, stat_rx[j, 0:1], stat_rx[j, 1:2]))
    _, mean, dev2 = merge(pieces)
    norm = coefficients(mean, dev2, gain2, bias2)

    def own_acts(i, c):
        activate_all(hid, 2, 2 + frames, i * ROWS, norm)
        return c

    lax.fori_loop(0, steps, own_acts, 0)
    close_top(2, 2 + frames)
    close_bottom(2, 2 + frames)
    for c in w_copies[6:]:
        c.wait()

    def edge_copies(p):
        first = last * (1 - p)
        two = pl.ds(first, 2)
        return (
            remote(send_d.at[two], recv_d.at[two], DOWN + p, 1, 0, 0),
            remote(send_c.at[two], recv_c.at[two], CORNER + p, 1, 1, 0),
            remote(send_r.at[two], recv_r.at[two], RIGHT + p, 0, 1, 0),
        )

    def decoded(first, r, rows, c, cols):
        parts = conv_block(wp2, first, r, rows, c, cols)
        at = pl.ds(r, rows)
        return [
            (first + o, part + tile[first + o + 2, at, c : c + cols].astype(F32))
            for o, part in enumerate(parts)
        ]

    def decoded_edges(first):
        base = lanes_of(first)
        acc = None
        for kh in range(3):
            lanes = pl.ds(base, 12 * chan)
            tall = acts[kh : kh + side, stride:side, lanes].reshape(side * OV, 12 * chan)
            low = acts[stride + kh : side + kh, 0:stride, lanes].reshape(stride * OV, 12 * chan)
            lhs = jnp.concatenate([tall, low], axis=0)
            part = jnp.dot(lhs, wp2[kh], preferred_element_type=F32)
            acc = part if acc is None else acc + part
        result = []
        for o in range(2):
            f = first + o
            mine = acc[:, o * chan : (o + 1) * chan]
            tall = mine[0 : side * OV].reshape(side, OV, chan)
            low = mine[side * OV :].reshape(OV, stride, chan)
            tall = tall + tile[f + 2, :, stride:side].astype(F32)
            low = low + tile[f + 2, stride:side, 0:stride].astype(F32)
            result.append((f, tall, low))
        return result

    def edges(p, carry):
        first = last * (1 - p)

        @pl.when(p == 1)
        def _():
            @pl.when(later)
            def _():
                for i in range(steps):
                    hid_copy(i).wait_recv()

            activate_early(hid, norm)

        d_copy, c_copy, r_copy = edge_copies(p)
        for f, tall, low in decoded_edges(first):
            send_r[f] = tall[0:stride].astype(BF16)
            send_c[f] = tall[stride:side].astype(BF16)
            send_d[f] = low.astype(BF16)
        when(has_right, r_copy.start)
        when(both_dr, c_copy.start)
        when(has_down, d_copy.start)
        return carry

    parts = stride // 24

    def interior(i, carry):
        first = last * (1 - lax.div(i, parts))
        r = lax.rem(i, parts) * 24
        for f, part in decoded(first, r, 24, 0, stride):
            out[f, pl.ds(r, 24)] = part.astype(BF16)
        return carry

    def interior_at(i):
        first = last * (1 - i)
        for f, part in decoded(first, 0, stride, 0, stride):
            out[f] = part.astype(BF16)

    ramp = lax.broadcasted_iota(jnp.int32, (1, OV, 1), 1).astype(F32) * (1.0 / OV)

    def blend(p):
        first = last * (1 - p)
        d_copy, c_copy, r_copy = edge_copies(p)
        when(has_up, d_copy.wait_recv)
        when(both_ul, c_copy.wait_recv)

        @pl.when(has_up)
        def _():
            for f in (first, first + 1):
                for i in range(OV):
                    t = i / OV
                    mix = recv_d[f, i].astype(F32) * (1.0 - t) + out[f, i].astype(F32) * t
                    out[f, i] = mix.astype(BF16)

        when(has_left, r_copy.wait_recv)

        @pl.when(both_ul)
        def _():
            for f in (first, first + 1):
                for i in range(OV):
                    t = i / OV
                    mix = recv_c[f, i].astype(F32) * (1.0 - t) + recv_r[f, i].astype(F32) * t
                    recv_r[f, i] = mix.astype(BF16)

        @pl.when(has_left)
        def _():
            for f in (first, first + 1):
                for r in range(0, stride, 8):
                    rows = slice(r, r + 8)
                    here = out[f, rows].astype(F32)
                    mix = recv_r[f, rows].astype(F32) * (1.0 - ramp) + here[:, 0:OV] * ramp
                    out[f, rows] = jnp.concatenate([mix, here[:, OV:]], axis=1).astype(BF16)

    lax.fori_loop(0, 2, edges, 0)
    interior_at(0)
    interior_at(1)
    blend(0)
    blend(1)

    for cond, c in sent:
        maybe(cond, c.wait_send)
    when(has_up, c_up.wait_send)
    when(can_lift, c_lift.wait_send)

    @pl.when(has_left)
    def _():
        for i in range(n_left):
            c_left(i).wait_send()

    @pl.when(has_next)
    def _():
        for i in range(3):
            c_prev(i).wait_send()
        for i in range(steps):
            hid_copy(i).wait_send()

    @pl.when(later)
    def _():
        when(has_up, r_up.wait_send)
        when(both_ul, r_diag.wait_send)
        when(has_left, r_left.wait_send)

    for c in s_copies:
        c.wait_send()
    for p in range(2):
        d_copy, c_copy, r_copy = edge_copies(p)
        when(has_down, d_copy.wait_send)
        when(both_dr, c_copy.wait_send)
        when(has_right, r_copy.wait_send)


def body(sizes, features, norm1_gain, norm1_bias, conv1_weight, norm2_gain, norm2_bias, conv2_weight):
    frames, stride, _, chan = features.shape
    side = stride + OV
    n_other = max(sizes[2] - 1, 1)
    vmem = pl.BlockSpec(memory_space=pltpu.VMEM)
    hbm = pl.BlockSpec(memory_space=pltpu.HBM)
    flat = lambda v: v.reshape(1, chan)
    taps = lambda w: w.reshape(3, 3, 3 * chan, chan)
    flops = 2 * 2 * frames * side * side * 27 * chan * chan
    result = pl.pallas_call(
        functools.partial(kernel, sizes),
        out_shape=pltpu.VMEM(features.shape, BF16),
        in_specs=[hbm] * 7,
        out_specs=vmem,
        scratch_shapes=[
            pltpu.VMEM((frames + 2, stride, stride, chan), BF16),
            pltpu.VMEM((frames + 2, OV, stride, chan), BF16),
            pltpu.VMEM((frames + 2, stride, OV, chan), BF16),
            pltpu.VMEM((frames + 2, OV, OV, chan), BF16),
            pltpu.VMEM((frames + 2, side, side, chan), BF16),
            pltpu.VMEM((side + 2, side, (frames + 2) * 3 * chan), BF16),
            pltpu.VMEM((frames + 2, side, side, chan), BF16),
            pltpu.VMEM((3, 12 * chan, 2 * chan), BF16),
            pltpu.VMEM((3, 12 * chan, 2 * chan), BF16),
            pltpu.VMEM((frames, OV, stride, chan), BF16),
            pltpu.VMEM((frames, stride, OV, chan), BF16),
            pltpu.VMEM((frames, OV, OV, chan), BF16),
            pltpu.VMEM((frames, OV, stride, chan), BF16),
            pltpu.VMEM((frames, stride, OV, chan), BF16),
            pltpu.VMEM((frames, OV, OV, chan), BF16),
            pltpu.VMEM((side // ROWS * 2, 8, chan), F32),
            pltpu.VMEM((side // ROWS * 2, 8, chan), F32),
            pltpu.VMEM((4, 8, chan), F32),
            pltpu.VMEM((sizes[2], 4, 8, chan), F32),
            pltpu.VMEM((8, chan), F32),
            pltpu.VMEM((n_other, 8, chan), F32),
            pltpu.SemaphoreType.DMA((N_SEM,)),
            pltpu.SemaphoreType.DMA((N_SEM,)),
            pltpu.SemaphoreType.DMA((sizes[2], 4)),
            pltpu.SemaphoreType.DMA((sizes[2], 4)),
            pltpu.SemaphoreType.DMA((n_other,)),
            pltpu.SemaphoreType.DMA((n_other,)),
            pltpu.SemaphoreType.DMA((12,)),
            pltpu.SemaphoreType.DMA,
            *[pltpu.VMEM((1, chan), F32) for _ in range(4)],
            pltpu.SemaphoreType.DMA((4,)),
        ],
        compiler_params=pltpu.CompilerParams(
            collective_id=0, has_side_effects=True, vmem_limit_bytes=40_000_000
        ),
        cost_estimate=pl.CostEstimate(
            flops=flops, bytes_accessed=4 << 20, transcendentals=12 * side * side * chan
        ),
    )(
        *[
            pltpu.with_memory_space_constraint(v, pltpu.HBM)
            for v in (
                features,
                flat(norm1_gain),
                flat(norm1_bias),
                taps(conv1_weight),
                flat(norm2_gain),
                flat(norm2_bias),
                taps(conv2_weight),
            )
        ]
    )
    return result


def solution(mesh):
    sizes = tuple(mesh.shape[a] for a in ("trow", "tcol", "span"))
    placed = (P("span", "trow", "tcol", None), P(), P(), P(), P(), P(), P())
    return jax.shard_map(
        functools.partial(body, sizes),
        mesh=mesh,
        in_specs=placed,
        out_specs=P("span", "trow", "tcol", None),
        check_vma=False,
    )
```
